32 devices in a mesh: dp: 2 (over y), ctx: 4 (over z), mp: 4 (over x, core).
Axes of the slice: x: 2, y: 2, z: 4, core: 2. Of those that a mesh axis runs over, the one named last changes fastest.
Arguments:
- hidden_in: bfloat16 [2, 4, 2048, 2048], P(None, 'dp', 'ctx'), may hold values from -6 to 6
- teacher: bfloat16 [2, 4, 2048, 2048], P(None, 'dp', 'ctx'), may hold values from -6 to 6
- lengths: int32 [2, 4], replicated, may hold values from 512 to 2048, as said below
- query_weight: bfloat16 [2048, 2048], P(('dp', 'ctx'), 'mp'), may hold values from -0.125 to 0.125
- key_weight: bfloat16 [2048, 2048], P(('dp', 'ctx'), 'mp'), may hold values from -0.125 to 0.125
- value_weight: bfloat16 [2048, 2048], P(('dp', 'ctx'), 'mp'), may hold values from -0.125 to 0.125
- out_weight: bfloat16 [2048, 2048], P('mp', ('dp', 'ctx')), may hold values from -2 to 2
- gate_weight: bfloat16 [2048, 5504], P(('dp', 'ctx'), 'mp'), may hold values from -0.125 to 0.125
- up_weight: bfloat16 [2048, 5504], P(('dp', 'ctx'), 'mp'), may hold values from -0.125 to 0.125
- down_weight: bfloat16 [5504, 2048], P('mp', ('dp', 'ctx')), may hold values from -0.078125 to 0.078125
- attention_gain: bfloat16 [2048], P(('dp', 'ctx')), may hold values from 0.25 to 1.75
- feed_gain: bfloat16 [2048], P(('dp', 'ctx')), may hold values from 0.25 to 1.75
Outputs:
- out_hidden: bfloat16 [2, 4, 2048, 2048], P(None, 'dp', 'ctx')
- loss: float32 [], replicated
- grad_hidden: bfloat16 [2, 4, 2048, 2048], P(None, 'dp', 'ctx')
- grad_query_weight: float32 [2048, 2048], P(('dp', 'ctx'), 'mp')
- grad_key_weight: float32 [2048, 2048], P(('dp', 'ctx'), 'mp')
- grad_value_weight: float32 [2048, 2048], P(('dp', 'ctx'), 'mp')
- grad_out_weight: float32 [2048, 2048], P('mp', ('dp', 'ctx'))
- grad_gate_weight: float32 [2048, 5504], P(('dp', 'ctx'), 'mp')
- grad_up_weight: float32 [2048, 5504], P(('dp', 'ctx'), 'mp')
- grad_down_weight: float32 [5504, 2048], P('mp', ('dp', 'ctx'))
- grad_attention_gain: float32 [2048], P(('dp', 'ctx'))
- grad_feed_gain: float32 [2048], P(('dp', 'ctx'))
The draws below stay inside these ranges and needn't reach their ends.
Inputs may be any that keep to these rules, and one draw needn't show every extreme that they name: Each micro-batch has one slot with all 2048 positions valid; the valid positions of a slot are its first lengths[m, s] ones.
All inputs are finite; a program needn't handle non-finite values.
Results may differ from the reference program's by a relative error of at most 0.012.
Values may be sent and summed in bfloat16 or wider, within the bound.
No kernel may reach another device: no remote copies, remote signals or barrier semaphores. Data moves between devices by JAX's collectives and lax.ppermute only.
A program may use at most 384 MiB of HBM per device.

```python
import jax
import jax.numpy as jnp
from jax import lax

D = 2048
HEADS = 16
HEAD_DIM = 128
FF = 5504
WINDOW = 1024
SEQ = 2048
MB = 2
SLOTS = 4


def draw_lengths(key, part):
    first, second = jax.random.split(jax.random.fold_in(key, 17))
    base = jax.random.randint(first, (MB, SLOTS), SEQ // 4, SEQ + 1)
    chosen = jax.random.randint(second, (MB, 1), 0, SLOTS)
    column = jnp.arange(SLOTS, dtype=jnp.int32)[None, :]
    return jnp.where(column == chosen, SEQ, base).astype(jnp.int32)


def shard_levels(own_key, dims, pieces, smallest, largest):
    factor_of = 1.0
    for axis_at, parts in pieces:
        heights = jax.random.uniform(jax.random.fold_in(jax.random.fold_in(own_key, 6), axis_at), (parts,), jnp.float32, smallest / len(pieces), largest / len(pieces))
        factor_of = factor_of * jnp.repeat(jnp.exp(heights), dims[axis_at] // parts).reshape((-1,) + (1,) * (len(dims) - 1 - axis_at))
    return factor_of


def normal_values(key, shape, scale, most, cuts=(), kind=jnp.bfloat16):
    level = shard_levels(key, shape, cuts, -0.22, 0.18) if cuts else 1.0
    entries = jax.random.normal(key, shape, jnp.float32) * scale * level
    return jnp.minimum(jnp.maximum(entries, -most), most).astype(kind)


def setup_inputs(seed: int = 0) -> dict:
    splits = jax.random.split(jax.random.key(seed), 13)
    hidden_in = normal_values(splits[0], (MB, SLOTS, SEQ, D), 1.0, 6.0, ((1, 2), (2, 4)))
    teacher = normal_values(splits[1], (MB, SLOTS, SEQ, D), 1.0, 6.0, ((1, 2), (2, 4)))
    lengths = draw_lengths(jax.random.fold_in(splits[12], 71), 0)
    query_weight = normal_values(splits[3], (D, HEADS * HEAD_DIM), D ** -0.5, 0.125, ((0, 8), (1, 4)))
    key_weight = normal_values(splits[4], (D, HEADS * HEAD_DIM), D ** -0.5, 0.125, ((0, 8), (1, 4)))
    value_weight = normal_values(splits[5], (D, HEADS * HEAD_DIM), D ** -0.5, 0.125, ((0, 8), (1, 4)))
    out_weight = normal_values(splits[6], (HEADS * HEAD_DIM, D), (max(HEADS * HEAD_DIM // 256, 1)) ** -0.5, 2.0, ((0, 4), (1, 8)))
    gate_weight = normal_values(splits[7], (D, FF), D ** -0.5, 0.125, ((0, 8), (1, 4)))
    up_weight = normal_values(splits[8], (D, FF), D ** -0.5, 0.125, ((0, 8), (1, 4)))
    down_weight = normal_values(splits[9], (FF, D), FF ** -0.5, 0.078125, ((0, 4), (1, 8)))
    attention_gain = jnp.clip(1.0 + 0.15 * jax.random.normal(splits[10], (D,), jnp.float32), 0.25, 1.75).astype(jnp.bfloat16)
    feed_gain = jnp.clip(1.0 + 0.15 * jax.random.normal(splits[11], (D,), jnp.float32), 0.25, 1.75).astype(jnp.bfloat16)
    return {"hidden_in": hidden_in, "teacher": teacher, "lengths": lengths, "query_weight": query_weight, "key_weight": key_weight, "value_weight": value_weight, "out_weight": out_weight, "gate_weight": gate_weight, "up_weight": up_weight, "down_weight": down_weight, "attention_gain": attention_gain, "feed_gain": feed_gain}


@jax.custom_vjp
def low(v):
    return lax.optimization_barrier(v.astype(jnp.bfloat16)).astype(jnp.float32)

@jax.custom_vjp
def low_back(v):
    return v

def low_keep(v):
    return (low(v), None)

def low_pass(kept, grad):
    return (grad,)

def back_keep(v):
    return (v, None)

def back_low(kept, grad):
    return (low(grad),)
low.defvjp(low_keep, low_pass)
low_back.defvjp(back_keep, back_low)
EPS = 1e-06
HIGH = lax.Precision.HIGHEST

def norm_rows(v):
    return v * lax.rsqrt(lax.optimization_barrier(jnp.mean(v * v, axis=-1, keepdims=True)) + EPS)

def silu(v):
    return v * jax.nn.sigmoid(v)

def matmul(left, right):
    return jnp.dot(left, right, precision=HIGH, preferred_element_type=jnp.float32)

def attention(queries, keys, values, length):
    block = min(512, SEQ)
    scale = HEAD_DIM ** (-0.5)
    padding = jnp.zeros((WINDOW, HEADS, HEAD_DIM), queries.dtype)
    keys_padded = jnp.concatenate([padding, keys], axis=0)
    values_padded = jnp.concatenate([padding, values], axis=0)

    def one_block(start):
        start = start.astype(jnp.int32)
        query_block = lax.dynamic_slice_in_dim(queries, start, block, 0)
        key_block = lax.dynamic_slice_in_dim(keys_padded, start, block + WINDOW, 0)
        value_block = lax.dynamic_slice_in_dim(values_padded, start, block + WINDOW, 0)
        query_pos = start + jnp.arange(block, dtype=jnp.int32)
        key_pos = start - WINDOW + jnp.arange(block + WINDOW, dtype=jnp.int32)
        distance = query_pos[:, None] - key_pos[None, :]
        allowed = (distance >= 0) & (distance < WINDOW) & (key_pos[None, :] >= 0)
        allowed = allowed & ((key_pos[None, :] < length) | (distance == 0))
        scores = low_back(jnp.einsum('qhd,khd->hqk', query_block, key_block, precision=HIGH) * scale)
        scores = jnp.where(allowed[None], scores, -1e+30)
        top = lax.optimization_barrier(jnp.max(scores, axis=-1, keepdims=True))
        expo = jnp.exp(scores - top)
        probs = expo / lax.optimization_barrier(jnp.sum(expo, axis=-1, keepdims=True))
        result = jnp.einsum('hqk,khd->qhd', low(probs), value_block, precision=HIGH)
        return low(low_back(result))
    starts = jnp.arange(SEQ // block, dtype=jnp.int32) * block
    blocks = lax.map(jax.checkpoint(one_block), starts)
    return blocks.reshape(SEQ, HEADS * HEAD_DIM)

def slot_layer(x_one, length, weights):
    w_query, w_key, w_value, w_out, w_gate, w_up, w_down, gain_a, gain_f = weights
    positions = jnp.arange(SEQ, dtype=jnp.int32)
    valid = (positions < length).astype(x_one.dtype)[:, None]
    normed_a = low(norm_rows(x_one) * gain_a)
    queries = low(low_back(matmul(normed_a, w_query))).reshape(SEQ, HEADS, HEAD_DIM)
    keys = low(low_back(matmul(normed_a, w_key))).reshape(SEQ, HEADS, HEAD_DIM)
    values = low(low_back(matmul(normed_a, w_value))).reshape(SEQ, HEADS, HEAD_DIM)
    attended = attention(queries, keys, values, length)
    mid = x_one + low_back(matmul(attended, w_out))
    normed_f = low(norm_rows(mid) * gain_f)
    gate = low_back(matmul(normed_f, w_gate))
    upper = low_back(matmul(normed_f, w_up))
    hidden = low(silu(gate) * upper)
    return (mid + low_back(matmul(hidden, w_down))) * valid

def reference(hidden_in, teacher, lengths, query_weight, key_weight, value_weight, out_weight, gate_weight, up_weight, down_weight, attention_gain, feed_gain):
    weights = tuple((w.astype(jnp.float32) for w in (query_weight, key_weight, value_weight, out_weight, gate_weight, up_weight, down_weight, attention_gain, feed_gain)))
    n_slots = MB * SLOTS
    inputs = hidden_in.astype(jnp.float32).reshape(n_slots, SEQ, D)
    targets = teacher.astype(jnp.float32).reshape(n_slots, SEQ, D)
    slot_lengths = lengths.reshape(n_slots).astype(jnp.int32)

    def total(inputs, weights):
        count = jnp.sum(slot_lengths).astype(inputs.dtype)

        def step(acc, item):
            x_one, t_one, len_one = item
            y_one = jax.checkpoint(slot_layer)(x_one, len_one, weights)
            valid = (jnp.arange(SEQ, dtype=jnp.int32) < len_one).astype(y_one.dtype)[:, None]
            error = (y_one - t_one) * valid
            return (acc + jnp.sum(error * error), y_one)
        acc, outs = lax.scan(step, jnp.zeros((), inputs.dtype), (inputs, targets, slot_lengths))
        return (acc / (count * D), outs)
    loss, pull, outs = jax.vjp(total, inputs, weights, has_aux=True)
    scale = 0.5 * n_slots * SEQ * D
    grad_x, grad_w = pull(jnp.ones_like(loss) * scale)
    out_hidden = outs.reshape(MB, SLOTS, SEQ, D).astype(jnp.bfloat16)
    grad_hidden = grad_x.reshape(MB, SLOTS, SEQ, D).astype(jnp.bfloat16)
    return (out_hidden, loss.astype(jnp.float32), grad_hidden, grad_w[0].astype(jnp.float32), grad_w[1].astype(jnp.float32), grad_w[2].astype(jnp.float32), grad_w[3].astype(jnp.float32), grad_w[4].astype(jnp.float32), grad_w[5].astype(jnp.float32), grad_w[6].astype(jnp.float32), grad_w[7].astype(jnp.float32), grad_w[8].astype(jnp.float32))
```

```python
import jax
import jax.numpy as jnp
from jax import lax
from jax.experimental import pallas as pl
from jax.experimental.pallas import tpu as pltpu
from jax.sharding import PartitionSpec as P

HEAD_DIM = 128
WINDOW = 1024
SEQ = 2048
EPS = 1e-06
NEGATIVE = -1e30
BF = jnp.bfloat16
F32 = jnp.float32


def dot_t(a, b, dims):
    return lax.dot_general(a, b, (dims, ((), ())), preferred_element_type=F32)


def plain_dot(left, right):
    return dot_t(left, right, ((1,), (0,)))


def left_dot(left, right):
    return dot_t(left, right, ((0,), (0,)))


def right_dot(left, right):
    return dot_t(left, right, ((1,), (1,)))


def masked_scores(q, k, behind, length, kcol, qrow, kbase):
    s = right_dot(k, q) * (HEAD_DIM**-0.5)
    valid = kcol + kbase < length
    if behind == 0:
        keep = (qrow >= jnp.where(valid, kcol, SEQ)) | (qrow == kcol)
    elif behind == 1:
        keep = jnp.broadcast_to(valid, s.shape)
    else:
        keep = qrow < jnp.where(valid, kcol, -1)
    return jnp.where(keep, s, NEGATIVE)


def piece(ref, block, rows):
    return ref[block * rows : (block + 1) * rows, :]


def attend_kernel(pair, per, back, len_ref, kcol_ref, qrow_ref, q_ref, *refs):
    n = (len(refs) - 2) // 2
    k_refs, v_refs, (o_ref, lse_ref) = refs[:n], refs[n : 2 * n], refs[2 * n :]
    rows = kcol_ref.shape[0]
    length = len_ref[0]
    kcol, qrow = kcol_ref[...], qrow_ref[...]
    base = (pair - n + 1) * per
    for b in range(per):
        chunk = pair * per + b
        seen = range(max(0, chunk - back), chunk + 1)
        where = [divmod(j - base, per) for j in seen]
        q = piece(q_ref, b, rows)
        scores = [
            masked_scores(q, piece(k_refs[p], i, rows), chunk - j, length, kcol, qrow, j * rows)
            for j, (p, i) in zip(seen, where)
        ]
        top = jnp.max(scores[0], axis=0, keepdims=True)
        for s in scores[1:]:
            top = jnp.maximum(top, jnp.max(s, axis=0, keepdims=True))
        expo = [jnp.exp(s - top) for s in scores]
        total = jnp.sum(expo[0], axis=0, keepdims=True)
        for e in expo[1:]:
            total = total + jnp.sum(e, axis=0, keepdims=True)
        inv = 1.0 / total
        out = jnp.zeros((HEAD_DIM, rows), F32)
        for e, (p, i) in zip(expo, where):
            out = out + left_dot(piece(v_refs[p], i, rows), (e * inv).astype(BF))
        o_ref[b * rows : (b + 1) * rows, :] = out.T.astype(BF)
        lse_ref[0, b : b + 1, :] = top + jnp.log(total)


def attend_back_kernel(pair, per, back, len_ref, kcol_ref, qrow_ref, q_ref, g_ref, lse_ref, *refs):
    n = (len(refs) - 1 + 2) // 6
    k_refs, v_refs = refs[:n], refs[n : 2 * n]
    in_refs = refs[2 * n : 4 * n - 2]
    gq_ref, out_refs = refs[4 * n - 2], refs[4 * n - 1 :]
    rows = kcol_ref.shape[0]
    length = len_ref[0]
    kcol, qrow = kcol_ref[...], qrow_ref[...]
    scale = HEAD_DIM**-0.5
    base = (pair - n + 1) * per
    sums = {}
    for b in range(per):
        chunk = pair * per + b
        seen = range(max(0, chunk - back), chunk + 1)
        where = [divmod(j - base, per) for j in seen]
        q, g = piece(q_ref, b, rows), piece(g_ref, b, rows)
        lse = lse_ref[0, b : b + 1, :]
        probs, gprobs = [], []
        inner = jnp.zeros((1, rows), F32)
        for j, (p, i) in zip(seen, where):
            s = masked_scores(q, piece(k_refs[p], i, rows), chunk - j, length, kcol, qrow, j * rows)
            e = jnp.exp(s - lse)
            ge = right_dot(piece(v_refs[p], i, rows), g)
            inner = inner + jnp.sum(e * ge, axis=0, keepdims=True)
            probs.append(e)
            gprobs.append(ge)
        gq = jnp.zeros((HEAD_DIM, rows), F32)
        for e, ge, at in zip(probs, gprobs, where):
            gs = (e * (ge - inner)).astype(BF)
            gq = gq + left_dot(piece(k_refs[at[0]], at[1], rows), gs)
            gk, gv = plain_dot(gs, q) * scale, plain_dot(e.astype(BF), g)
            if at in sums:
                gk, gv = gk + sums[at][0], gv + sums[at][1]
            sums[at] = (gk, gv)
        gq_ref[b * rows : (b + 1) * rows, :] = (gq.T * scale).astype(BF)
    for p in range(n):
        for i in range(per):
            at = slice(i * rows, (i + 1) * rows)
            for which in range(2):
                out_ref = out_refs[which * n + p]
                value = sums[p, i][which] if (p, i) in sums else None
                if p < n - 1:
                    before = in_refs[which * (n - 1) + p][at, :]
                    value = before if value is None else value + before
                out_ref[at, :] = value.astype(out_ref.dtype)


def attend_call(kernel, name, pair, per, back, kcol, qrow, length, ins, lses, shapes, n_dots):
    rows = kcol.shape[0]
    wide, cols = ins[0].shape
    heads = cols // HEAD_DIM
    block = pl.BlockSpec((wide, HEAD_DIM), lambda h, *_: (0, h))
    lse_block = pl.BlockSpec((1, per, rows), lambda h, *_: (h, 0, 0))
    blocks = sum(min(pair * per + b, back) + 1 for b in range(per))
    n_lse = len(lses)
    return pl.pallas_call(
        lambda *refs: kernel(pair, per, back, *refs),
        grid_spec=pltpu.PrefetchScalarGridSpec(
            num_scalar_prefetch=1,
            grid=(heads,),
            in_specs=[
                pl.BlockSpec((rows, 1), lambda h, *_: (0, 0)),
                pl.BlockSpec((1, rows), lambda h, *_: (0, 0)),
            ]
            + ([block] * 2 + [lse_block] + [block] * (len(ins) - 2) if lses else [block] * len(ins)),
            out_specs=[block if shape.ndim == 2 else lse_block for shape in shapes],
        ),
        out_shape=shapes,
        compiler_params=pltpu.CompilerParams(vmem_limit_bytes=56 << 20),
        cost_estimate=pl.CostEstimate(
            flops=6 * n_dots * blocks * rows * rows * HEAD_DIM * heads,
            bytes_accessed=2 * wide * cols * (len(ins) + len(shapes)),
            transcendentals=blocks * rows * rows * heads,
        ),
        name=f"{name}{pair}",
    )(length, kcol, qrow, *((*ins[:2], *lses, *ins[2:]) if lses else ins))


def core_swap(v):
    return lax.ppermute(v, "mp", [(i, i ^ 1) for i in range(4)])


def chip_swap(v):
    return lax.ppermute(v, "mp", [(i, i ^ 2) for i in range(4)])


def dp_swap(v):
    return lax.ppermute(v, "dp", [(i, i ^ 1) for i in range(2)])


def ctx_turn(v, steps):
    n = lax.axis_size("ctx")
    return lax.ppermute(v, "ctx", [(i, (i + steps) % n) for i in range(n)])


def after(value, *others):
    return lax.optimization_barrier((value, *others))[0]


def pick(v, index):
    return lax.dynamic_index_in_dim(v, index, 0, keepdims=False)


def join(got, own):
    return jnp.concatenate([own, got], axis=1)


def join_flat(got, own):
    return join(got, own).reshape(-1, own.shape[2])


class Order:
    def __init__(self):
        self.last = ()

    def __call__(self, step, first, *rest):
        if self.last:
            first = after(first, *self.last)
        out = step(first, *rest)
        self.last = (jax.tree.leaves(out)[0],)
        return out

    def wait(self, *values):
        self.last = (*self.last, *values)


def split_part(part, per):
    part = part.reshape(per, -1, part.shape[1])
    return part[:, part.shape[1] // 2 :].astype(BF), part


def add_core(got, keep):
    mine = keep[:, : keep.shape[1] // 2] + got.astype(F32)
    half = mine.shape[1] // 2
    return mine[:, half:].astype(BF), mine[:, :half]


def own_first(v, y):
    half = v.shape[-1] // 2
    return jnp.where(y == 0, v, jnp.concatenate([v[..., half:], v[..., :half]], axis=-1))


def whole_part(right, left):
    return left_dot(left, right)


def whole_rest(right, left, part):
    return (part + left_dot(left, right)).astype(BF)


def their_part(right, left):
    return left_dot(left[:, left.shape[1] // 2 :], right)


def their_rest(right, left, part):
    return (part + their_part(right, left)).astype(BF)


def own_part_grad(right, left):
    return left_dot(left[:, : left.shape[1] // 2], right)


def own_rest(right, left, part, got):
    return (part + own_part_grad(right, left) + got.astype(F32)).astype(BF)


def both_scatter(grad):
    halves = grad.reshape(2, -1, grad.shape[1])
    return lax.psum_scatter(halves, "ctx", scatter_dimension=1, tiled=True)


def ring_scatter(grad, z):
    n = lax.axis_size("ctx")
    blocks = grad.reshape(n, -1, grad.shape[1])
    travel = pick(blocks, (z + n - 1) % n)
    for k in range(2, n + 1):
        total = pick(blocks, (z + n - k) % n).astype(F32) + ctx_turn(travel, 1).astype(F32)
        travel = total.astype(BF)
    return total


def to_slots(v, z):
    n = v.shape[0]
    return [pick(v, z)] + [ctx_turn(pick(v, (z + k) % n), k) for k in range(1, n)]


def place_kernel(index_ref, *refs):
    step = pl.program_id(0)
    for i, ref in enumerate(refs[:-1]):

        @pl.when(step == i)
        def _(ref=ref):
            refs[-1][0, 0] = ref[...]


def whole_rows(blocks, index, n):
    rows, width = blocks[0].shape
    return pl.pallas_call(
        place_kernel,
        grid_spec=pltpu.PrefetchScalarGridSpec(
            num_scalar_prefetch=1,
            grid=(len(blocks),),
            in_specs=[
                pl.BlockSpec((rows, width), lambda i, _: (0, 0), pipeline_mode=pl.Buffered(1))
            ]
            * len(blocks),
            out_specs=pl.BlockSpec((1, 1, rows, width), lambda i, at: (at[i, 0], at[i, 1], 0, 0)),
        ),
        out_shape=jax.ShapeDtypeStruct((n, 4, rows, width), blocks[0].dtype),
        compiler_params=pltpu.CompilerParams(vmem_limit_bytes=24 << 20),
        cost_estimate=pl.CostEstimate(
            flops=0, bytes_accessed=4 * len(blocks) * rows * width, transcendentals=0
        ),
        name="place_rows",
    )(jnp.stack([jnp.stack(at) for at in index]).astype(jnp.int32), *blocks)


def all_sum(v):
    v = v + core_swap(v)
    v = v + chip_swap(v)
    v = v + dp_swap(v)
    n = lax.axis_size("ctx")
    step = 1
    while step < n:
        v = v + lax.ppermute(v, "ctx", [(i, i ^ step) for i in range(n)])
        step *= 2
    return v


def norm_scale(v):
    return lax.rsqrt(jnp.mean(v * v, axis=-1, keepdims=True) + EPS)


def norm_back(v, r, gain, grad):
    z = v * r
    e = grad * gain
    return r * (e - z * jnp.mean(e * z, axis=-1, keepdims=True)), jnp.sum(grad * z, axis=(0, 1))


def slot_device(
    hidden_in,
    teacher,
    lengths,
    query_weight,
    key_weight,
    value_weight,
    out_weight,
    gate_weight,
    up_weight,
    down_weight,
    attention_gain,
    feed_gain,
):
    n_micro, n_slot, group, width = hidden_in.shape
    n_chunk = n_micro * n_slot
    quarter = group // 4
    cols = query_weight.shape[1]
    heads = cols // HEAD_DIM
    back = WINDOW // group
    ctx_index = lax.axis_index("ctx")
    dp_index = lax.axis_index("dp")
    mp_index = lax.axis_index("mp")
    core_index, x_index = mp_index % 2, mp_index // 2
    place = core_index * 2 + x_index
    share = attention_gain.shape[0]
    count = jnp.sum(lengths).astype(F32)
    factor = lengths.shape[0] * lengths.shape[1] * SEQ / count
    length = lax.dynamic_slice(
        lengths, (ctx_index // n_slot, dp_index * n_slot + ctx_index % n_slot), (1, 1)
    ).reshape(1)
    row = jnp.arange(group, dtype=jnp.int32)
    inside = ((row // quarter) ^ place) * quarter + row % quarter
    kcol, qrow = inside[:, None], inside[None, :]
    own_inside = place * quarter + jnp.arange(quarter, dtype=jnp.int32)
    chunks = range(n_chunk)

    def own_part(v):
        v = lax.dynamic_slice_in_dim(v.reshape(n_chunk, group, width), place * quarter, quarter, 1)
        return to_slots(own_first(v, dp_index), ctx_index)

    def by_chunk(parts):
        parts = jnp.stack(parts)
        return [pick(parts, (ctx_index - c) % n_chunk) for c in chunks]

    x_parts = own_part(hidden_in)
    x_peers = [chip_swap(part) for part in x_parts]
    x_pairs = [jnp.concatenate(pair, axis=0) for pair in zip(x_parts, x_peers)]
    x_cores = [core_swap(pair) for pair in x_pairs]
    x_own = by_chunk(x_parts)
    x_all = by_chunk([jnp.concatenate(pair, axis=0) for pair in zip(x_pairs, x_cores)])
    gain_rows = jnp.pad(jnp.stack([attention_gain, feed_gain]), ((0, 14), (0, cols - share)))
    shards = [
        jnp.concatenate([query_weight, gain_rows], axis=0),
        key_weight,
        value_weight,
        out_weight.T,
        gate_weight,
        up_weight,
    ]
    parts = []
    for i, shard in enumerate(shards):
        if i > 0:
            shard = after(shard, *x_parts, *parts[-2:-1])
        parts.append(lax.all_gather(shard, "ctx", axis=0, tiled=True))
    shard = after(down_weight.T, *x_parts, *parts[-2:-1])
    part_down = [
        lax.all_gather(v, "ctx", axis=0, tiled=True) for v in (shard, dp_swap(down_weight.T))
    ]
    w_down = jnp.concatenate(part_down, axis=0)
    gates = [x_parts, x_peers, x_cores] + [()] * 3
    fetched = [(part, dp_swap(after(part, *gate))) for part, gate in zip(parts, gates)]
    query_parts = [part.reshape(n_chunk, share + 16, cols) for part in fetched[0]]
    fetched[0] = [part[:, :share].reshape(n_chunk * share, cols) for part in query_parts]
    gain_a, gain_f = [
        jnp.concatenate([part[:, share + i, :share].reshape(-1) for part in query_parts]).astype(F32)
        for i in range(2)
    ]
    part_gate, part_up = parts[4:]
    w_query, w_key, w_value, w_out, w_gate, w_up = [
        jnp.concatenate(pair, axis=0) for pair in fetched
    ]
    teacher_parts = own_part(after(teacher, part_up))
    target = by_chunk(teacher_parts)
    per = 2
    pairs = range(n_chunk // per)
    x_own = [jnp.stack(x_own[p * per : (p + 1) * per]) for p in pairs]
    target = [jnp.stack(target[p * per : (p + 1) * per]) for p in pairs]
    order = Order()
    reach = -(-back // per)
    mid, r_f, sent, kept = [], [], {}, {}

    def gather_half(own):
        return order(join, chip_swap(own), own)

    def gather_rest(pair):
        return order(join_flat, core_swap(pair), pair)

    def pass_core(p):
        sent[p], kept[p] = order(add_core, core_swap(sent[p]), kept[p])

    h1, queries, keys, values, attended, lse, h2 = [], [], [], [], [], [], []

    def project(h):
        return [plain_dot(h, w).astype(BF) for w in (w_query, w_key, w_value)]

    def normed(*xs):
        x = jnp.concatenate(xs, axis=0).astype(F32)
        return (x * norm_scale(x) * gain_a).astype(BF)

    def attention(p):
        first = max(0, p - reach)

        def step(q):
            ins = [q, *keys[first : p + 1], *values[first : p + 1]]
            shapes = [
                jax.ShapeDtypeStruct(q.shape, BF),
                jax.ShapeDtypeStruct((heads, per, group), F32),
            ]
            return attend_call(
                attend_kernel, "attend", p, per, back, kcol, qrow, length, ins, [], shapes, 4
            )

        a, l = order(step, queries[p])
        attended.append(a)
        lse.append(l)

    def enter_feed(p):
        def step(got, keep, x):
            v = x.astype(F32) + (keep + got.astype(F32))
            r = norm_scale(v)
            return (v * r * gain_f).astype(BF), v, r

        low, v, r = order(step, chip_swap(sent[p]), kept[p], x_own[p])
        mid.append(v)
        r_f.append(r)
        return low

    for p in pairs:
        h1.append(order(normed, *x_all[p * per : (p + 1) * per]))
    for p in pairs:
        q, k, v = order(project, h1[p])
        queries.append(q)
        keys.append(k)
        values.append(v)
        order.wait((parts[3], part_gate)[p])
        attention(p)
        sent[p], kept[p] = order(lambda a: split_part(right_dot(a, w_out), per), attended[p])
    pass_core(0)
    pass_core(1)
    low = [enter_feed(0)]
    order.wait(part_up, fetched[4][1])
    low.append(enter_feed(1))
    low[0] = gather_half(low[0])
    order.wait(fetched[5][1])
    low[1] = gather_half(low[1])
    h2 += [gather_rest(v) for v in low]

    gate, up, hidden, results, g_result, g_branch, loss_parts = [], [], [], [], [], [], []

    def unit(h):
        g, u = plain_dot(h, w_gate), plain_dot(h, w_up)
        return (g * jax.nn.sigmoid(g) * u).astype(BF), g, u

    def finish(p):
        def step(got, keep, v, t):
            at = (p * per + jnp.arange(per, dtype=jnp.int32))[:, None] * group + own_inside
            valid = (at < length)[:, :, None].astype(F32)
            result = (v + (keep + got.astype(F32))) * valid
            error = (result - t.astype(F32)) * valid
            grad = error * factor
            return grad.astype(BF), grad, result.astype(BF), jnp.sum(error * error)

        low, grad, result, loss = order(step, chip_swap(sent[p]), kept[p], mid[p], target[p])
        results.append(result)
        g_result.append(grad)
        loss_parts.append(loss)
        return low

    for p in pairs:
        h, g, u = order(unit, h2[p])
        hidden.append(h)
        gate.append(g)
        up.append(u)
        if p == 0:
            order.wait(*teacher_parts)
    for p in pairs:
        sent[p], kept[p] = order(lambda h: split_part(right_dot(h, w_down), per), hidden[p])
    pass_core(0)
    pass_core(1)
    low = [finish(0), finish(1)]
    low[0] = gather_half(low[0])
    g_branch.append(gather_rest(low[0]))

    g_gate, g_up, g_mid, g_att, gain_f_parts = [], [], [], [], []

    def leave_unit(p):
        def step(g_out, g, u):
            g_hidden = plain_dot(g_out, w_down)
            sig = jax.nn.sigmoid(g)
            return (
                (g_hidden * g * sig).astype(BF),
                (g_hidden * u * sig * (1.0 + g * (1.0 - sig))).astype(BF),
            )

        gu, gg = order(step, g_branch[p], gate[p], up[p])
        g_up.append(gu)
        g_gate.append(gg)

    def project_unit(p):
        def step(gg, gu):
            return split_part(right_dot(gg, w_gate) + right_dot(gu, w_up), per)

        sent[p], kept[p] = order(step, g_gate[p], g_up[p])

    def enter_attention(p):
        def step(got, keep, v, r, grad):
            g_norm, g_gain = norm_back(v, r, gain_f, keep + got.astype(F32))
            total = grad + g_norm
            return total.astype(BF), total, g_gain

        low, total, g_gain = order(step, chip_swap(sent[p]), kept[p], mid[p], r_f[p], g_result[p])
        g_mid.append(total)
        gain_f_parts.append(g_gain)
        return low

    scattered = []

    def scatter(rights, lefts, got):
        part = order(own_part_grad, rights[0], lefts[0])
        own = order(own_rest, rights[1], lefts[1], part, got)
        scattered.append(ring_scatter(own, ctx_index))

    def send(rights, lefts):
        part = order(their_part, rights[0], lefts[0])
        return dp_swap(order(their_rest, rights[1], lefts[1], part))

    part = order(whole_part, hidden[0], g_branch[0])
    leave_unit(0)
    low[1] = gather_half(low[1])
    gate_part = order(whole_part, g_gate[0], h2[0])
    g_branch.append(gather_rest(low[1]))
    d_down = order(whole_rest, hidden[1], g_branch[1], part)
    s_down = both_scatter(d_down)
    leave_unit(1)
    s_gate = both_scatter(order(whole_rest, g_gate[1], h2[1], gate_part))
    up_part = order(whole_part, g_up[0], h2[0])
    s_up = both_scatter(order(whole_rest, g_up[1], h2[1], up_part))
    project_unit(0)
    pass_core(0)
    project_unit(1)
    pass_core(1)
    low = [enter_attention(0), enter_attention(1)]
    low[0] = gather_half(low[0])
    g_att.append(gather_rest(low[0]))

    g_q, g_k, g_v = [None] * len(pairs), [None] * len(pairs), [None] * len(pairs)
    g_in, gain_a_parts = [], []

    def attention_back(p):
        first = max(0, p - reach)
        last = p == len(pairs) - 1

        def step(g):
            ins = [queries[p], plain_dot(g, w_out).astype(BF), *keys[first : p + 1], *values[first : p + 1]]
            kinds = [BF if last or p - j == reach else F32 for j in range(first, p + 1)]
            shape = ins[0].shape
            shapes = [jax.ShapeDtypeStruct(shape, kind) for kind in [BF] + kinds * 2]
            return attend_call(
                attend_back_kernel, "attend_back", p, per, back, kcol, qrow, length,
                [*ins, *g_k[first:p], *g_v[first:p]], [lse[p]], shapes, 10,
            )

        out = order(step, g_att[p])
        n = p - first + 1
        g_q[p] = out[0]
        g_k[first : p + 1] = out[1 : 1 + n]
        g_v[first : p + 1] = out[1 + n :]

    def project_back(p):
        def step(q, k, v):
            whole = right_dot(q, w_query) + right_dot(k, w_key) + right_dot(v, w_value)
            return split_part(whole, per)

        sent[p], kept[p] = order(step, g_q[p], g_k[p], g_v[p])

    def leave(p):
        def step(got, keep, x, grad):
            x = x.astype(F32)
            g_norm, g_gain = norm_back(x, norm_scale(x), gain_a, keep + got.astype(F32))
            return (grad + g_norm).astype(BF), g_gain

        low, g_gain = order(step, chip_swap(sent[p]), kept[p], x_own[p], g_mid[p])
        g_in.append(low)
        gain_a_parts.append(g_gain)

    attention_back(0)
    low[1] = gather_half(low[1])
    g_att.append(gather_rest(low[1]))
    results = [after(v, low[1]) for v in results]
    out_parts = to_slots(own_first(jnp.concatenate(results, axis=0), dp_index), ctx_index)
    out_got = send(attended, g_att)
    attention_back(1)
    order.wait(s_gate)
    project_back(0)
    project_back(1)
    out_own = order(lambda first, *rest: jnp.stack([first, *rest]), *out_parts)
    out_peer, out_core = chip_swap(out_own), core_swap(out_own)
    pass_core(0)
    got = [send(g_q, h1)]
    pass_core(1)
    got += [send(right, h1) for right in (g_k, g_v)]
    leave(0)
    leave(1)
    back_parts = to_slots(own_first(jnp.concatenate(g_in, axis=0), dp_index), ctx_index)
    scatter(attended, g_att, out_got)
    slots = [(ctx_index - k) % n_chunk for k in chunks]
    index = [(slot, place ^ i) for slot in slots for i in range(4)]

    def place_out(own, *others):
        blocks = [v[k] for k in chunks for v in (own, *others)]
        return whole_rows(blocks, index, n_chunk)

    scatter(g_q, h1, got[0])
    out_hidden = order(place_out, out_own, out_peer, out_core, core_swap(out_peer))
    scatter(g_k, h1, got[1])
    scatter(g_v, h1, got[2])
    back_blocks = []
    for own in back_parts:
        peer = chip_swap(own)
        back_blocks += [own, peer, core_swap(own), core_swap(peer)]
    grad_hidden = order(lambda first, *rest: whole_rows([first, *rest], index, n_chunk), *back_blocks)
    grad_down, grad_gate, grad_up = [
        v[0].astype(F32) + dp_swap(v[1]).astype(F32)
        for v in (after(v, *g_in) for v in (s_down, s_gate, s_up))
    ]
    gain_a_part, gain_f_part, loss_part = sum(gain_a_parts), sum(gain_f_parts), sum(loss_parts)
    small = jnp.concatenate(
        [own_first(gain_a_part, dp_index), own_first(gain_f_part, dp_index), jnp.full((128,), loss_part)]
    )
    small = all_sum(small.reshape(-1, 128)).reshape(-1)
    at = (dp_index * n_chunk + ctx_index) * share
    shape = hidden_in.shape
    return (
        out_hidden.reshape(shape),
        small[2 * width] / (count * width),
        grad_hidden.reshape(shape),
        *scattered[1:],
        scattered[0].T,
        grad_gate,
        grad_up,
        grad_down.T,
        lax.dynamic_slice_in_dim(small, at, share),
        lax.dynamic_slice_in_dim(small, width + at, share),
    )


def shifted(value, axis, steps):
    count = lax.axis_size(axis)
    leading, last = (max(0, -steps), min(count, count - steps))
    return lax.ppermute(value, axis, [(source, source + steps) for source in range(leading, last)])


def norm_rows(v):
    return v * lax.rsqrt(jnp.mean(v * v, axis=-1, keepdims=True) + EPS)


def silu(v):
    return v * jax.nn.sigmoid(v)


def gain_norm(values, gain):
    return norm_rows(values) * gain


def gated_unit(gate, upper):
    return silu(gate) * upper


def on_device(
    hidden_in,
    teacher,
    lengths,
    query_weight,
    key_weight,
    value_weight,
    out_weight,
    gate_weight,
    up_weight,
    down_weight,
    attention_gain,
    feed_gain,
):
    n_micro, n_slot, group, width = hidden_in.shape
    local_heads = query_weight.shape[1] // HEAD_DIM
    head_cols = query_weight.shape[1]
    reach = WINDOW // group
    extent = (reach + 1) * group
    rows = n_slot * group
    scale = HEAD_DIM ** (-0.5)
    ctx_index = lax.axis_index("ctx")
    dp_index = lax.axis_index("dp")
    count = jnp.sum(lengths).astype(jnp.float32)
    factor = lengths.shape[0] * lengths.shape[1] * SEQ / count
    own_lengths = lax.dynamic_slice_in_dim(lengths, dp_index * n_slot, n_slot, 1)
    positions = ctx_index * group + jnp.arange(group, dtype=jnp.int32)
    key_positions = ctx_index * group - reach * group + jnp.arange(extent, dtype=jnp.int32)
    distance = positions[:, None] - key_positions[None, :]
    in_window = (distance >= 0) & (distance < WINDOW) & (key_positions[None, :] >= 0)

    def fetch_attention():
        return (
            lax.all_gather(query_weight, ("dp", "ctx"), axis=0, tiled=True),
            lax.all_gather(key_weight, ("dp", "ctx"), axis=0, tiled=True),
            lax.all_gather(value_weight, ("dp", "ctx"), axis=0, tiled=True),
            lax.all_gather(out_weight, ("dp", "ctx"), axis=1, tiled=True),
            lax.all_gather(attention_gain, ("dp", "ctx"), axis=0, tiled=True),
        )

    def fetch_feed():
        return (
            lax.all_gather(gate_weight, ("dp", "ctx"), axis=0, tiled=True),
            lax.all_gather(up_weight, ("dp", "ctx"), axis=0, tiled=True),
            lax.all_gather(down_weight, ("dp", "ctx"), axis=1, tiled=True),
            lax.all_gather(feed_gain, ("dp", "ctx"), axis=0, tiled=True),
        )

    acc_query = jnp.zeros((width, head_cols), jnp.float32)
    acc_key = jnp.zeros((width, head_cols), jnp.float32)
    acc_value = jnp.zeros((width, head_cols), jnp.float32)
    acc_out = jnp.zeros((head_cols, width), jnp.float32)
    acc_gate = jnp.zeros((width, gate_weight.shape[1]), jnp.float32)
    acc_up = jnp.zeros((width, gate_weight.shape[1]), jnp.float32)
    acc_down = jnp.zeros((gate_weight.shape[1], width), jnp.float32)
    acc_gain_a = jnp.zeros((width,), jnp.float32)
    acc_gain_f = jnp.zeros((width,), jnp.float32)
    loss_part = jnp.zeros((), jnp.float32)
    results = []
    input_grads = []

    def scores_of(queries_four, keys_ext, allowed):
        raw = (
            jnp.einsum(
                "sqhd,skhd->shqk", queries_four, keys_ext, preferred_element_type=jnp.float32
            )
            * scale
        )
        return jnp.where(allowed[:, None], raw, NEGATIVE)

    for micro in range(n_micro):
        slot_len = own_lengths[micro]
        valid = positions[None, :] < slot_len[:, None]
        key_ok = (key_positions[None, None, :] < slot_len[:, None, None]) | (distance == 0)[None]
        allowed = in_window[None] & key_ok
        valid_rows = valid.reshape(rows, 1).astype(jnp.float32)
        attention_set = fetch_attention()
        full_query, full_key, full_value, full_out, full_gain_a = attention_set
        gain_a = full_gain_a.astype(jnp.float32)
        x_in = hidden_in[micro].reshape(rows, width).astype(jnp.float32)
        normed_a = gain_norm(x_in, gain_a).astype(jnp.bfloat16)
        queries = plain_dot(normed_a, full_query).astype(jnp.bfloat16)
        keys = plain_dot(normed_a, full_key).astype(jnp.bfloat16)
        values = plain_dot(normed_a, full_value).astype(jnp.bfloat16)
        keys_slot = keys.reshape(n_slot, group, head_cols)
        values_slot = values.reshape(n_slot, group, head_cols)
        key_parts = []
        value_parts = []
        for back in range(reach, 0, -1):
            got_keys, got_values = shifted((keys_slot, values_slot), "ctx", back)
            key_parts.append(got_keys)
            value_parts.append(got_values)
        keys_ext = jnp.concatenate(key_parts + [keys_slot], axis=1).reshape(
            n_slot, extent, local_heads, HEAD_DIM
        )
        values_ext = jnp.concatenate(value_parts + [values_slot], axis=1).reshape(
            n_slot, extent, local_heads, HEAD_DIM
        )
        queries_four = queries.reshape(n_slot, group, local_heads, HEAD_DIM)
        scores = scores_of(queries_four, keys_ext, allowed)
        top = jnp.max(scores, axis=-1, keepdims=True)
        expo = jnp.exp(scores - top)
        summed = jnp.sum(expo, axis=-1, keepdims=True)
        logsum = top + jnp.log(summed)
        probs = (expo / summed).astype(jnp.bfloat16)
        attended = jnp.einsum(
            "shqk,skhd->sqhd", probs, values_ext, preferred_element_type=jnp.float32
        )
        attended = attended.astype(jnp.bfloat16).reshape(rows, head_cols)
        branch_a = lax.psum(plain_dot(attended, full_out), "mp")
        mid = x_in + branch_a
        feed_set = fetch_feed()
        full_gate, full_up, full_down, full_gain_f = feed_set
        gain_f = full_gain_f.astype(jnp.float32)
        normed_f = gain_norm(mid, gain_f).astype(jnp.bfloat16)
        gate_val = plain_dot(normed_f, full_gate)
        up_val = plain_dot(normed_f, full_up)
        hidden_units = gated_unit(gate_val, up_val).astype(jnp.bfloat16)
        branch_f = lax.psum(plain_dot(hidden_units, full_down), "mp")
        result = (mid + branch_f) * valid_rows
        target = teacher[micro].reshape(rows, width).astype(jnp.float32)
        error = (result - target) * valid_rows
        loss_part = loss_part + jnp.sum(error * error)
        results.append(result.astype(jnp.bfloat16).reshape(n_slot, group, width))
        back_feed = fetch_feed()
        full_gate, full_up, full_down, full_gain_f = back_feed
        grad_result = error * factor
        grad_branch = grad_result.astype(jnp.bfloat16)
        acc_down = acc_down + left_dot(hidden_units, grad_branch)
        grad_units = right_dot(grad_branch, full_down)
        unused, pull_unit = jax.vjp(gated_unit, gate_val, up_val)
        grad_gate, grad_upper = pull_unit(grad_units)
        grad_gate = grad_gate.astype(jnp.bfloat16)
        grad_upper = grad_upper.astype(jnp.bfloat16)
        acc_gate = acc_gate + left_dot(normed_f, grad_gate)
        acc_up = acc_up + left_dot(normed_f, grad_upper)
        grad_normed_f = lax.psum(
            right_dot(grad_gate, full_gate) + right_dot(grad_upper, full_up), "mp"
        )
        unused, pull_norm = jax.vjp(gain_norm, mid, gain_f)
        grad_mid_norm, grad_gain_f = pull_norm(grad_normed_f)
        acc_gain_f = acc_gain_f + grad_gain_f
        grad_mid = grad_result + grad_mid_norm
        back_attention = fetch_attention()
        full_query, full_key, full_value, full_out, full_gain_a = back_attention
        grad_att = grad_mid.astype(jnp.bfloat16)
        acc_out = acc_out + left_dot(attended, grad_att)
        grad_attended = (
            right_dot(grad_att, full_out)
            .astype(jnp.bfloat16)
            .reshape(n_slot, group, local_heads, HEAD_DIM)
        )
        scores_again = scores_of(queries_four, keys_ext, allowed)
        probs_back = jnp.exp(scores_again - logsum)
        grad_values_ext = jnp.einsum(
            "shqk,sqhd->skhd",
            probs_back.astype(jnp.bfloat16),
            grad_attended,
            preferred_element_type=jnp.float32,
        )
        grad_probs = jnp.einsum(
            "sqhd,skhd->shqk", grad_attended, values_ext, preferred_element_type=jnp.float32
        )
        inner = jnp.sum(probs_back * grad_probs, axis=-1, keepdims=True)
        grad_scores = (probs_back * (grad_probs - inner)).astype(jnp.bfloat16)
        grad_queries = (
            jnp.einsum("shqk,skhd->sqhd", grad_scores, keys_ext, preferred_element_type=jnp.float32)
            * scale
        )
        grad_keys_ext = (
            jnp.einsum(
                "shqk,sqhd->skhd", grad_scores, queries_four, preferred_element_type=jnp.float32
            )
            * scale
        )
        grad_keys_ext = grad_keys_ext.reshape(n_slot, extent, head_cols)
        grad_values_ext = grad_values_ext.reshape(n_slot, extent, head_cols)
        grad_keys_total = grad_keys_ext[:, reach * group :]
        grad_values_total = grad_values_ext[:, reach * group :]
        for back in range(1, reach + 1):
            offset = (reach - back) * group
            piece_keys = grad_keys_ext[:, offset : offset + group]
            piece_values = grad_values_ext[:, offset : offset + group]
            got_keys, got_values = shifted((piece_keys, piece_values), "ctx", -back)
            grad_keys_total = grad_keys_total + got_keys
            grad_values_total = grad_values_total + got_values
        grad_queries = grad_queries.reshape(rows, head_cols).astype(jnp.bfloat16)
        grad_keys_low = grad_keys_total.reshape(rows, head_cols).astype(jnp.bfloat16)
        grad_values_low = grad_values_total.reshape(rows, head_cols).astype(jnp.bfloat16)
        acc_query = acc_query + left_dot(normed_a, grad_queries)
        acc_key = acc_key + left_dot(normed_a, grad_keys_low)
        acc_value = acc_value + left_dot(normed_a, grad_values_low)
        grad_normed_a = (
            right_dot(grad_queries, full_query)
            + right_dot(grad_keys_low, full_key)
            + right_dot(grad_values_low, full_value)
        )
        grad_normed_a = lax.psum(grad_normed_a, "mp")
        unused, pull_first = jax.vjp(gain_norm, x_in, gain_a)
        grad_x_norm, grad_gain_a = pull_first(grad_normed_a)
        acc_gain_a = acc_gain_a + grad_gain_a
        grad_in = grad_mid + grad_x_norm
        input_grads.append(grad_in.astype(jnp.bfloat16).reshape(n_slot, group, width))
    loss = lax.psum(loss_part, ("dp", "ctx")) / (count * width)
    grads = (
        lax.psum_scatter(acc_query, ("dp", "ctx"), scatter_dimension=0, tiled=True),
        lax.psum_scatter(acc_key, ("dp", "ctx"), scatter_dimension=0, tiled=True),
        lax.psum_scatter(acc_value, ("dp", "ctx"), scatter_dimension=0, tiled=True),
        lax.psum_scatter(acc_out, ("dp", "ctx"), scatter_dimension=1, tiled=True),
        lax.psum_scatter(acc_gate, ("dp", "ctx"), scatter_dimension=0, tiled=True),
        lax.psum_scatter(acc_up, ("dp", "ctx"), scatter_dimension=0, tiled=True),
        lax.psum_scatter(acc_down, ("dp", "ctx"), scatter_dimension=1, tiled=True),
        lax.psum_scatter(acc_gain_a, ("dp", "ctx"), scatter_dimension=0, tiled=True),
        lax.psum_scatter(acc_gain_f, ("dp", "ctx"), scatter_dimension=0, tiled=True),
    )
    return (
        jnp.stack(results),
        loss,
        jnp.stack(input_grads),
        grads[0],
        grads[1],
        grads[2],
        grads[3],
        grads[4],
        grads[5],
        grads[6],
        grads[7],
        grads[8],
    )


def solution(mesh):
    in_specs = (
        P(None, "dp", "ctx", None),
        P(None, "dp", "ctx", None),
        P(),
        P(("dp", "ctx"), "mp"),
        P(("dp", "ctx"), "mp"),
        P(("dp", "ctx"), "mp"),
        P("mp", ("dp", "ctx")),
        P(("dp", "ctx"), "mp"),
        P(("dp", "ctx"), "mp"),
        P("mp", ("dp", "ctx")),
        P(("dp", "ctx")),
        P(("dp", "ctx")),
    )
    out_specs = (
        P(None, "dp", "ctx", None),
        P(),
        P(None, "dp", "ctx", None),
        P(("dp", "ctx"), "mp"),
        P(("dp", "ctx"), "mp"),
        P(("dp", "ctx"), "mp"),
        P("mp", ("dp", "ctx")),
        P(("dp", "ctx"), "mp"),
        P(("dp", "ctx"), "mp"),
        P("mp", ("dp", "ctx")),
        P(("dp", "ctx")),
        P(("dp", "ctx")),
    )
    slots = 8 // mesh.shape["dp"]
    whole_slots = mesh.shape["ctx"] == slots and mesh.shape["mp"] == 4
    return jax.shard_map(
        slot_device if whole_slots else on_device, mesh=mesh, in_specs=in_specs, out_specs=out_specs, check_vma=False
    )
```

```python
import jax
import jax.numpy as jnp
from jax import lax
from jax.experimental import pallas as pl
from jax.experimental.pallas import tpu as pltpu
from jax.sharding import PartitionSpec as P

HEAD_DIM = 128
WINDOW = 1024
SEQ = 2048
EPS = 1e-06
NEGATIVE = -1e30
BF = jnp.bfloat16
F32 = jnp.float32


def dot_t(a, b, dims):
    return lax.dot_general(a, b, (dims, ((), ())), preferred_element_type=F32)


def plain_dot(left, right):
    return dot_t(left, right, ((1,), (0,)))


def left_dot(left, right):
    return dot_t(left, right, ((0,), (0,)))


def right_dot(left, right):
    return dot_t(left, right, ((1,), (1,)))


def masked_scores(q, k, behind, length, kcol, qrow, kbase):
    s = right_dot(k, q) * (HEAD_DIM**-0.5)
    valid = kcol + kbase < length
    if behind == 0:
        keep = (qrow >= jnp.where(valid, kcol, SEQ)) | (qrow == kcol)
    elif behind == 1:
        keep = jnp.broadcast_to(valid, s.shape)
    else:
        keep = qrow < jnp.where(valid, kcol, -1)
    return jnp.where(keep, s, NEGATIVE)


def piece(ref, block, rows):
    return ref[block * rows : (block + 1) * rows, :]


def attend_kernel(pair, per, back, len_ref, kcol_ref, qrow_ref, q_ref, *refs):
    n = (len(refs) - 2) // 2
    k_refs, v_refs, (o_ref, lse_ref) = refs[:n], refs[n : 2 * n], refs[2 * n :]
    rows = kcol_ref.shape[0]
    length = len_ref[0]
    kcol, qrow = kcol_ref[...], qrow_ref[...]
    base = (pair - n + 1) * per
    for b in range(per):
        chunk = pair * per + b
        seen = range(max(0, chunk - back), chunk + 1)
        where = [divmod(j - base, per) for j in seen]
        q = piece(q_ref, b, rows)
        scores = [
            masked_scores(q, piece(k_refs[p], i, rows), chunk - j, length, kcol, qrow, j * rows)
            for j, (p, i) in zip(seen, where)
        ]
        top = jnp.max(scores[0], axis=0, keepdims=True)
        for s in scores[1:]:
            top = jnp.maximum(top, jnp.max(s, axis=0, keepdims=True))
        expo = [jnp.exp(s - top) for s in scores]
        total = jnp.sum(expo[0], axis=0, keepdims=True)
        for e in expo[1:]:
            total = total + jnp.sum(e, axis=0, keepdims=True)
        inv = 1.0 / total
        out = jnp.zeros((HEAD_DIM, rows), F32)
        for e, (p, i) in zip(expo, where):
            out = out + left_dot(piece(v_refs[p], i, rows), (e * inv).astype(BF))
        o_ref[b * rows : (b + 1) * rows, :] = out.T.astype(BF)
        lse_ref[0, b : b + 1, :] = top + jnp.log(total)


def attend_back_kernel(pair, per, back, len_ref, kcol_ref, qrow_ref, q_ref, g_ref, lse_ref, *refs):
    n = (len(refs) - 1 + 2) // 6
    k_refs, v_refs = refs[:n], refs[n : 2 * n]
    in_refs = refs[2 * n : 4 * n - 2]
    gq_ref, out_refs = refs[4 * n - 2], refs[4 * n - 1 :]
    rows = kcol_ref.shape[0]
    length = len_ref[0]
    kcol, qrow = kcol_ref[...], qrow_ref[...]
    scale = HEAD_DIM**-0.5
    base = (pair - n + 1) * per
    sums = {}
    for b in range(per):
        chunk = pair * per + b
        seen = range(max(0, chunk - back), chunk + 1)
        where = [divmod(j - base, per) for j in seen]
        q, g = piece(q_ref, b, rows), piece(g_ref, b, rows)
        lse = lse_ref[0, b : b + 1, :]
        probs, gprobs = [], []
        inner = jnp.zeros((1, rows), F32)
        for j, (p, i) in zip(seen, where):
            s = masked_scores(q, piece(k_refs[p], i, rows), chunk - j, length, kcol, qrow, j * rows)
            e = jnp.exp(s - lse)
            ge = right_dot(piece(v_refs[p], i, rows), g)
            inner = inner + jnp.sum(e * ge, axis=0, keepdims=True)
            probs.append(e)
            gprobs.append(ge)
        gq = jnp.zeros((HEAD_DIM, rows), F32)
        for e, ge, at in zip(probs, gprobs, where):
            gs = (e * (ge - inner)).astype(BF)
            gq = gq + left_dot(piece(k_refs[at[0]], at[1], rows), gs)
            gk, gv = plain_dot(gs, q) * scale, plain_dot(e.astype(BF), g)
            if at in sums:
                gk, gv = gk + sums[at][0], gv + sums[at][1]
            sums[at] = (gk, gv)
        gq_ref[b * rows : (b + 1) * rows, :] = (gq.T * scale).astype(BF)
    for p in range(n):
        for i in range(per):
            at = slice(i * rows, (i + 1) * rows)
            for which in range(2):
                out_ref = out_refs[which * n + p]
                value = sums[p, i][which] if (p, i) in sums else None
                if p < n - 1:
                    before = in_refs[which * (n - 1) + p][at, :]
                    value = before if value is None else value + before
                out_ref[at, :] = value.astype(out_ref.dtype)


def attend_call(kernel, name, pair, per, back, kcol, qrow, length, ins, lses, shapes, n_dots):
    rows = kcol.shape[0]
    wide, cols = ins[0].shape
    heads = cols // HEAD_DIM
    block = pl.BlockSpec((wide, HEAD_DIM), lambda h, *_: (0, h))
    lse_block = pl.BlockSpec((1, per, rows), lambda h, *_: (h, 0, 0))
    blocks = sum(min(pair * per + b, back) + 1 for b in range(per))
    n_lse = len(lses)
    return pl.pallas_call(
        lambda *refs: kernel(pair, per, back, *refs),
        grid_spec=pltpu.PrefetchScalarGridSpec(
            num_scalar_prefetch=1,
            grid=(heads,),
            in_specs=[
                pl.BlockSpec((rows, 1), lambda h, *_: (0, 0)),
                pl.BlockSpec((1, rows), lambda h, *_: (0, 0)),
            ]
            + ([block] * 2 + [lse_block] + [block] * (len(ins) - 2) if lses else [block] * len(ins)),
            out_specs=[block if shape.ndim == 2 else lse_block for shape in shapes],
        ),
        out_shape=shapes,
        compiler_params=pltpu.CompilerParams(vmem_limit_bytes=56 << 20),
        cost_estimate=pl.CostEstimate(
            flops=n_dots * blocks * rows * rows * HEAD_DIM * heads,
            bytes_accessed=1 << 16 if lses else 2 * wide * cols * (len(ins) + len(shapes)),
            transcendentals=0 if lses else blocks * rows * rows * heads,
        ),
        name=f"{name}{pair}",
    )(length, kcol, qrow, *((*ins[:2], *lses, *ins[2:]) if lses else ins))


def core_swap(v):
    return lax.ppermute(v, "mp", [(i, i ^ 1) for i in range(4)])


def chip_swap(v):
    return lax.ppermute(v, "mp", [(i, i ^ 2) for i in range(4)])


def dp_swap(v):
    return lax.ppermute(v, "dp", [(i, i ^ 1) for i in range(2)])


def ctx_turn(v, steps):
    n = lax.axis_size("ctx")
    return lax.ppermute(v, "ctx", [(i, (i + steps) % n) for i in range(n)])


def after(value, *others):
    return lax.optimization_barrier((value, *others))[0]


def pick(v, index):
    return lax.dynamic_index_in_dim(v, index, 0, keepdims=False)


def join(got, own):
    return jnp.concatenate([own, got], axis=1)


def join_flat(got, own):
    return join(got, own).reshape(-1, own.shape[2])


class Order:
    def __init__(self):
        self.last = ()

    def __call__(self, step, first, *rest):
        if self.last:
            first = after(first, *self.last)
        out = step(first, *rest)
        self.last = (jax.tree.leaves(out)[0],)
        return out

    def wait(self, *values):
        self.last = (*self.last, *values)


def split_part(part, per):
    part = part.reshape(per, -1, part.shape[1])
    return part[:, part.shape[1] // 2 :].astype(BF), part


def add_core(got, keep):
    mine = keep[:, : keep.shape[1] // 2] + got.astype(F32)
    half = mine.shape[1] // 2
    return mine[:, half:].astype(BF), mine[:, :half]


def own_first(v, y):
    half = v.shape[-1] // 2
    return jnp.where(y == 0, v, jnp.concatenate([v[..., half:], v[..., :half]], axis=-1))


def whole_part(right, left):
    return left_dot(left, right)


def whole_rest(right, left, part):
    return (part + left_dot(left, right)).astype(BF)


def their_part(right, left):
    return left_dot(left[:, left.shape[1] // 2 :], right)


def their_rest(right, left, part):
    return (part + their_part(right, left)).astype(BF)


def own_part_grad(right, left):
    return left_dot(left[:, : left.shape[1] // 2], right)


def own_rest(right, left, part, got):
    return (part + own_part_grad(right, left) + got.astype(F32)).astype(BF)


def both_scatter(grad):
    half = grad.shape[0] // 2
    swapped = jnp.concatenate([grad[half:], grad[:half]], axis=0)
    grad = jnp.where(lax.axis_index("dp") == 0, grad, swapped)
    return lax.psum_scatter(grad, ("dp", "ctx"), scatter_dimension=0, tiled=True)


def to_slots(v, z):
    n = v.shape[0]
    return [pick(v, z)] + [ctx_turn(pick(v, (z + k) % n), k) for k in range(1, n)]


def place_kernel(index_ref, *refs):
    step = pl.program_id(0)
    for i, ref in enumerate(refs[:-1]):

        @pl.when(step == i)
        def _(ref=ref):
            refs[-1][0, 0] = ref[...]


def whole_rows(blocks, index, n):
    rows, width = blocks[0].shape
    return pl.pallas_call(
        place_kernel,
        grid_spec=pltpu.PrefetchScalarGridSpec(
            num_scalar_prefetch=1,
            grid=(len(blocks),),
            in_specs=[
                pl.BlockSpec((rows, width), lambda i, _: (0, 0), pipeline_mode=pl.Buffered(1))
            ]
            * len(blocks),
            out_specs=pl.BlockSpec((1, 1, rows, width), lambda i, at: (at[i, 0], at[i, 1], 0, 0)),
        ),
        out_shape=jax.ShapeDtypeStruct((n, 4, rows, width), blocks[0].dtype),
        compiler_params=pltpu.CompilerParams(vmem_limit_bytes=24 << 20),
        cost_estimate=pl.CostEstimate(
            flops=0, bytes_accessed=4 * len(blocks) * rows * width, transcendentals=0
        ),
        name="place_rows",
    )(jnp.stack([jnp.stack(at) for at in index]).astype(jnp.int32), *blocks)


def all_sum(v):
    v = v + core_swap(v)
    v = v + chip_swap(v)
    v = v + dp_swap(v)
    n = lax.axis_size("ctx")
    step = 1
    while step < n:
        v = v + lax.ppermute(v, "ctx", [(i, i ^ step) for i in range(n)])
        step *= 2
    return v


def norm_scale(v):
    return lax.rsqrt(jnp.mean(v * v, axis=-1, keepdims=True) + EPS)


def norm_back(v, r, gain, grad):
    z = v * r
    e = grad * gain
    return r * (e - z * jnp.mean(e * z, axis=-1, keepdims=True)), jnp.sum(grad * z, axis=(0, 1))


def slot_device(
    hidden_in,
    teacher,
    lengths,
    query_weight,
    key_weight,
    value_weight,
    out_weight,
    gate_weight,
    up_weight,
    down_weight,
    attention_gain,
    feed_gain,
):
    n_micro, n_slot, group, width = hidden_in.shape
    n_chunk = n_micro * n_slot
    quarter = group // 4
    cols = query_weight.shape[1]
    heads = cols // HEAD_DIM
    back = WINDOW // group
    ctx_index = lax.axis_index("ctx")
    dp_index = lax.axis_index("dp")
    mp_index = lax.axis_index("mp")
    core_index, x_index = mp_index % 2, mp_index // 2
    place = core_index * 2 + x_index
    share = attention_gain.shape[0]
    count = jnp.sum(lengths).astype(F32)
    factor = lengths.shape[0] * lengths.shape[1] * SEQ / count
    length = lax.dynamic_slice(
        lengths, (ctx_index // n_slot, dp_index * n_slot + ctx_index % n_slot), (1, 1)
    ).reshape(1)
    row = jnp.arange(group, dtype=jnp.int32)
    inside = ((row // quarter) ^ place) * quarter + row % quarter
    kcol, qrow = inside[:, None], inside[None, :]
    own_inside = place * quarter + jnp.arange(quarter, dtype=jnp.int32)
    chunks = range(n_chunk)

    def own_part(v):
        v = lax.dynamic_slice_in_dim(v.reshape(n_chunk, group, width), place * quarter, quarter, 1)
        return to_slots(own_first(v, dp_index), ctx_index)

    def by_chunk(parts):
        parts = jnp.stack(parts)
        return [pick(parts, (ctx_index - c) % n_chunk) for c in chunks]

    x_parts = own_part(hidden_in)
    x_peers = [chip_swap(part) for part in x_parts]
    x_pairs = [jnp.concatenate(pair, axis=0) for pair in zip(x_parts, x_peers)]
    x_cores = [core_swap(pair) for pair in x_pairs]
    x_own = by_chunk(x_parts)
    x_all = by_chunk([jnp.concatenate(pair, axis=0) for pair in zip(x_pairs, x_cores)])
    gain_rows = jnp.pad(jnp.stack([attention_gain, feed_gain]), ((0, 14), (0, cols - share)))
    shards = [
        jnp.concatenate([query_weight, gain_rows], axis=0),
        key_weight,
        value_weight,
        out_weight.T,
        gate_weight,
        up_weight,
    ]
    parts = []
    for i, shard in enumerate(shards):
        if i > 0:
            shard = after(shard, *x_parts, *parts[-2:-1])
        parts.append(lax.all_gather(shard, "ctx", axis=0, tiled=True))
    shard = after(down_weight.T, *x_parts, *parts[-2:-1])
    part_down = [
        lax.all_gather(v, "ctx", axis=0, tiled=True) for v in (shard, dp_swap(down_weight.T))
    ]
    w_down = jnp.concatenate(part_down, axis=0)
    gates = [x_parts, x_peers, x_cores] + [()] * 3
    fetched = [(part, dp_swap(after(part, *gate))) for part, gate in zip(parts, gates)]
    query_parts = [part.reshape(n_chunk, share + 16, cols) for part in fetched[0]]
    fetched[0] = [part[:, :share].reshape(n_chunk * share, cols) for part in query_parts]
    gain_a, gain_f = [
        jnp.concatenate([part[:, share + i, :share].reshape(-1) for part in query_parts]).astype(F32)
        for i in range(2)
    ]
    part_gate, part_up = parts[4:]
    w_query, w_key, w_value, w_out, w_gate, w_up = [
        jnp.concatenate(pair, axis=0) for pair in fetched
    ]
    teacher_parts = own_part(after(teacher, part_up))
    target = by_chunk(teacher_parts)
    per = 2
    pairs = range(n_chunk // per)
    x_own = [jnp.stack(x_own[p * per : (p + 1) * per]) for p in pairs]
    target = [jnp.stack(target[p * per : (p + 1) * per]) for p in pairs]
    order = Order()
    reach = -(-back // per)
    mid, r_f, sent, kept = [], [], {}, {}

    def gather_half(own):
        return order(join, chip_swap(own), own)

    def gather_rest(pair):
        return order(join_flat, core_swap(pair), pair)

    def pass_core(p):
        sent[p], kept[p] = order(add_core, core_swap(sent[p]), kept[p])

    h1, queries, keys, values, attended, lse, h2 = [], [], [], [], [], [], []

    def project(h):
        return [plain_dot(h, w).astype(BF) for w in (w_query, w_key, w_value)]

    def normed(*xs):
        x = jnp.concatenate(xs, axis=0).astype(F32)
        return (x * norm_scale(x) * gain_a).astype(BF)

    def attention(p):
        first = max(0, p - reach)

        def step(q):
            ins = [q, *keys[first : p + 1], *values[first : p + 1]]
            shapes = [
                jax.ShapeDtypeStruct(q.shape, BF),
                jax.ShapeDtypeStruct((heads, per, group), F32),
            ]
            return attend_call(
                attend_kernel, "attend", p, per, back, kcol, qrow, length, ins, [], shapes, 24
            )

        a, l = order(step, queries[p])
        attended.append(a)
        lse.append(l)

    def enter_feed(p):
        def step(got, keep, x):
            v = x.astype(F32) + (keep + got.astype(F32))
            r = norm_scale(v)
            return (v * r * gain_f).astype(BF), v, r

        low, v, r = order(step, chip_swap(sent[p]), kept[p], x_own[p])
        mid.append(v)
        r_f.append(r)
        return low

    for p in pairs:
        h1.append(order(normed, *x_all[p * per : (p + 1) * per]))
    for p in pairs:
        q, k, v = order(project, h1[p])
        queries.append(q)
        keys.append(k)
        values.append(v)
        order.wait((parts[3], part_gate)[p])
        attention(p)
        sent[p], kept[p] = order(lambda a: split_part(right_dot(a, w_out), per), attended[p])
    pass_core(0)
    pass_core(1)
    order.wait(fetched[4][1])
    low = [enter_feed(0)]
    order.wait(part_up)
    low.append(enter_feed(1))
    low = [gather_half(v) for v in low]
    order.wait(fetched[5][1])
    h2.append(gather_rest(low[0]))

    gate, up, hidden, results, g_result, g_branch, loss_parts = [], [], [], [], [], [], []

    def unit(h):
        g, u = plain_dot(h, w_gate), plain_dot(h, w_up)
        return (g * jax.nn.sigmoid(g) * u).astype(BF), g, u

    def finish(p):
        def step(got, keep, v, t):
            at = (p * per + jnp.arange(per, dtype=jnp.int32))[:, None] * group + own_inside
            valid = (at < length)[:, :, None].astype(F32)
            result = (v + (keep + got.astype(F32))) * valid
            error = (result - t.astype(F32)) * valid
            grad = error * factor
            return grad.astype(BF), grad, result.astype(BF), jnp.sum(error * error)

        low, grad, result, loss = order(step, chip_swap(sent[p]), kept[p], mid[p], target[p])
        results.append(result)
        g_result.append(grad)
        loss_parts.append(loss)
        return low

    def feed(p):
        h, g, u = order(unit, h2[p])
        hidden.append(h)
        gate.append(g)
        up.append(u)

    def project_down(p):
        sent[p], kept[p] = order(lambda h: split_part(right_dot(h, w_down), per), hidden[p])

    g_gate, g_up, g_mid, g_att, gain_f_parts = [], [], [], [], []

    def leave_unit(p):
        def step(g_out, g, u):
            g_hidden = plain_dot(g_out, w_down)
            sig = jax.nn.sigmoid(g)
            return (
                (g_hidden * g * sig).astype(BF),
                (g_hidden * u * sig * (1.0 + g * (1.0 - sig))).astype(BF),
            )

        gu, gg = order(step, g_branch[p], gate[p], up[p])
        g_up.append(gu)
        g_gate.append(gg)

    def project_unit(p):
        def step(gg, gu):
            return split_part(right_dot(gg, w_gate) + right_dot(gu, w_up), per)

        sent[p], kept[p] = order(step, g_gate[p], g_up[p])

    def enter_attention(p):
        def step(got, keep, v, r, grad):
            g_norm, g_gain = norm_back(v, r, gain_f, keep + got.astype(F32))
            total = grad + g_norm
            return total.astype(BF), total, g_gain

        low, total, g_gain = order(step, chip_swap(sent[p]), kept[p], mid[p], r_f[p], g_result[p])
        g_mid.append(total)
        gain_f_parts.append(g_gain)
        return low

    scattered = []

    def scatter(rights, lefts, got):
        part = order(own_part_grad, rights[0], lefts[0])
        own = order(own_rest, rights[1], lefts[1], part, got)
        scattered.append(lax.psum_scatter(own, "ctx", scatter_dimension=0, tiled=True))

    def send(rights, lefts):
        part = order(their_part, rights[0], lefts[0])
        return dp_swap(order(their_rest, rights[1], lefts[1], part))

    g_q, g_k, g_v = [None] * len(pairs), [None] * len(pairs), [None] * len(pairs)
    g_in, gain_a_parts = [], []

    def attention_back(p):
        first = max(0, p - reach)
        last = p == len(pairs) - 1

        def step(g):
            ins = [queries[p], plain_dot(g, w_out).astype(BF), *keys[first : p + 1], *values[first : p + 1]]
            kinds = [BF if last or p - j == reach else F32 for j in range(first, p + 1)]
            shape = ins[0].shape
            shapes = [jax.ShapeDtypeStruct(shape, kind) for kind in [BF] + kinds * 2]
            return attend_call(
                attend_back_kernel, "attend_back", p, per, back, kcol, qrow, length,
                [*ins, *g_k[first:p], *g_v[first:p]], [lse[p]], shapes, 0,
            )

        out = order(step, g_att[p])
        n = p - first + 1
        g_q[p] = out[0]
        g_k[first : p + 1] = out[1 : 1 + n]
        g_v[first : p + 1] = out[1 + n :]

    def project_back(p):
        def step(q, k, v):
            whole = right_dot(q, w_query) + right_dot(k, w_key) + right_dot(v, w_value)
            return split_part(whole, per)

        sent[p], kept[p] = order(step, g_q[p], g_k[p], g_v[p])

    def leave(p):
        def step(got, keep, x, grad):
            x = x.astype(F32)
            g_norm, g_gain = norm_back(x, norm_scale(x), gain_a, keep + got.astype(F32))
            return (grad + g_norm).astype(BF), g_gain

        low, g_gain = order(step, chip_swap(sent[p]), kept[p], x_own[p], g_mid[p])
        g_in.append(low)
        gain_a_parts.append(g_gain)

    feed(0)
    order.wait(*teacher_parts)
    project_down(0)
    h2.append(gather_rest(low[1]))
    pass_core(0)
    feed(1)
    first = finish(0)
    project_down(1)
    pass_core(1)
    g_branch.append(gather_rest(gather_half(first)))
    leave_unit(0)
    part = order(whole_part, hidden[0], g_branch[0])
    second = finish(1)
    out_parts = to_slots(own_first(jnp.concatenate(results, axis=0), dp_index), ctx_index)
    project_unit(0)
    pass_core(0)
    order.wait(*out_parts)
    g_branch.append(gather_rest(gather_half(second)))
    leave_unit(1)
    s_down = both_scatter(order(whole_rest, hidden[1], g_branch[1], part))
    first = enter_attention(0)
    project_unit(1)
    pass_core(1)
    part = order(whole_part, g_gate[0], h2[0])
    s_gate = both_scatter(order(whole_rest, g_gate[1], h2[1], part))
    g_att.append(gather_rest(gather_half(first)))
    attention_back(0)
    order.wait(s_down)
    second = enter_attention(1)
    g_att.append(gather_rest(gather_half(second)))
    part = order(whole_part, g_up[0], h2[0])
    s_up = both_scatter(order(whole_rest, g_up[1], h2[1], part))
    out_got = send(attended, g_att)
    out_own = order(lambda first, *rest: jnp.stack([first, *rest]), *out_parts)
    out_peer, out_core = chip_swap(out_own), core_swap(out_own)
    attention_back(1)
    order.wait(out_peer, out_got)
    project_back(0)
    pass_core(0)
    rights = [
        order(lambda q, k, v: jnp.concatenate([q, k, v], axis=1), g_q[p], g_k[p], g_v[p]) for p in pairs
    ]
    qkv_got = send(rights, h1)
    order.wait(s_gate)
    project_back(1)
    leave(0)
    pass_core(1)
    leave(1)
    back_parts = to_slots(own_first(jnp.concatenate(g_in, axis=0), dp_index), ctx_index)
    scatter(attended, g_att, out_got)
    part = order(own_part_grad, rights[0], h1[0])
    slots = [(ctx_index - k) % n_chunk for k in chunks]
    index = [(slot, place ^ i) for slot in slots for i in range(4)]

    def place_out(own, *others):
        blocks = [v[k] for k in chunks for v in (own, *others)]
        return whole_rows(blocks, index, n_chunk)

    order.wait(*back_parts, qkv_got)
    out_hidden = order(place_out, out_own, out_peer, out_core, core_swap(out_peer))
    back_peers = [chip_swap(own) for own in back_parts]
    order.wait(s_up, *back_peers)
    own = order(own_rest, rights[1], h1[1], part, qkv_got)
    s_qkv = lax.psum_scatter(own, "ctx", scatter_dimension=0, tiled=True).astype(F32)
    back_blocks = []
    for own, peer in zip(back_parts, back_peers):
        back_blocks += [own, peer, core_swap(own), core_swap(peer)]
    grad_hidden = order(lambda first, *rest: whole_rows([first, *rest], index, n_chunk), *back_blocks)
    grad_down, grad_gate, grad_up = [v.astype(F32) for v in (s_down, s_gate, s_up)]
    gain_a_part, gain_f_part, loss_part = sum(gain_a_parts), sum(gain_f_parts), sum(loss_parts)
    small = jnp.concatenate(
        [own_first(gain_a_part, dp_index), own_first(gain_f_part, dp_index), jnp.full((128,), loss_part)]
    )
    small = all_sum(after(small, *back_peers).reshape(-1, 128)).reshape(-1)
    at = (dp_index * n_chunk + ctx_index) * share
    shape = hidden_in.shape
    return (
        out_hidden.reshape(shape),
        small[2 * width] / (count * width),
        grad_hidden.reshape(shape),
        s_qkv[:, :cols],
        s_qkv[:, cols : 2 * cols],
        s_qkv[:, 2 * cols :],
        scattered[0].astype(F32).T,
        grad_gate,
        grad_up,
        grad_down.T,
        lax.dynamic_slice_in_dim(small, at, share),
        lax.dynamic_slice_in_dim(small, width + at, share),
    )


def shifted(value, axis, steps):
    count = lax.axis_size(axis)
    leading, last = (max(0, -steps), min(count, count - steps))
    return lax.ppermute(value, axis, [(source, source + steps) for source in range(leading, last)])


def norm_rows(v):
    return v * lax.rsqrt(jnp.mean(v * v, axis=-1, keepdims=True) + EPS)


def silu(v):
    return v * jax.nn.sigmoid(v)


def gain_norm(values, gain):
    return norm_rows(values) * gain


def gated_unit(gate, upper):
    return silu(gate) * upper


def on_device(
    hidden_in,
    teacher,
    lengths,
    query_weight,
    key_weight,
    value_weight,
    out_weight,
    gate_weight,
    up_weight,
    down_weight,
    attention_gain,
    feed_gain,
):
    n_micro, n_slot, group, width = hidden_in.shape
    local_heads = query_weight.shape[1] // HEAD_DIM
    head_cols = query_weight.shape[1]
    reach = WINDOW // group
    extent = (reach + 1) * group
    rows = n_slot * group
    scale = HEAD_DIM ** (-0.5)
    ctx_index = lax.axis_index("ctx")
    dp_index = lax.axis_index("dp")
    count = jnp.sum(lengths).astype(jnp.float32)
    factor = lengths.shape[0] * lengths.shape[1] * SEQ / count
    own_lengths = lax.dynamic_slice_in_dim(lengths, dp_index * n_slot, n_slot, 1)
    positions = ctx_index * group + jnp.arange(group, dtype=jnp.int32)
    key_positions = ctx_index * group - reach * group + jnp.arange(extent, dtype=jnp.int32)
    distance = positions[:, None] - key_positions[None, :]
    in_window = (distance >= 0) & (distance < WINDOW) & (key_positions[None, :] >= 0)

    def fetch_attention():
        return (
            lax.all_gather(query_weight, ("dp", "ctx"), axis=0, tiled=True),
            lax.all_gather(key_weight, ("dp", "ctx"), axis=0, tiled=True),
            lax.all_gather(value_weight, ("dp", "ctx"), axis=0, tiled=True),
            lax.all_gather(out_weight, ("dp", "ctx"), axis=1, tiled=True),
            lax.all_gather(attention_gain, ("dp", "ctx"), axis=0, tiled=True),
        )

    def fetch_feed():
        return (
            lax.all_gather(gate_weight, ("dp", "ctx"), axis=0, tiled=True),
            lax.all_gather(up_weight, ("dp", "ctx"), axis=0, tiled=True),
            lax.all_gather(down_weight, ("dp", "ctx"), axis=1, tiled=True),
            lax.all_gather(feed_gain, ("dp", "ctx"), axis=0, tiled=True),
        )

    acc_query = jnp.zeros((width, head_cols), jnp.float32)
    acc_key = jnp.zeros((width, head_cols), jnp.float32)
    acc_value = jnp.zeros((width, head_cols), jnp.float32)
    acc_out = jnp.zeros((head_cols, width), jnp.float32)
    acc_gate = jnp.zeros((width, gate_weight.shape[1]), jnp.float32)
    acc_up = jnp.zeros((width, gate_weight.shape[1]), jnp.float32)
    acc_down = jnp.zeros((gate_weight.shape[1], width), jnp.float32)
    acc_gain_a = jnp.zeros((width,), jnp.float32)
    acc_gain_f = jnp.zeros((width,), jnp.float32)
    loss_part = jnp.zeros((), jnp.float32)
    results = []
    input_grads = []

    def scores_of(queries_four, keys_ext, allowed):
        raw = (
            jnp.einsum(
                "sqhd,skhd->shqk", queries_four, keys_ext, preferred_element_type=jnp.float32
            )
            * scale
        )
        return jnp.where(allowed[:, None], raw, NEGATIVE)

    for micro in range(n_micro):
        slot_len = own_lengths[micro]
        valid = positions[None, :] < slot_len[:, None]
        key_ok = (key_positions[None, None, :] < slot_len[:, None, None]) | (distance == 0)[None]
        allowed = in_window[None] & key_ok
        valid_rows = valid.reshape(rows, 1).astype(jnp.float32)
        attention_set = fetch_attention()
        full_query, full_key, full_value, full_out, full_gain_a = attention_set
        gain_a = full_gain_a.astype(jnp.float32)
        x_in = hidden_in[micro].reshape(rows, width).astype(jnp.float32)
        normed_a = gain_norm(x_in, gain_a).astype(jnp.bfloat16)
        queries = plain_dot(normed_a, full_query).astype(jnp.bfloat16)
        keys = plain_dot(normed_a, full_key).astype(jnp.bfloat16)
        values = plain_dot(normed_a, full_value).astype(jnp.bfloat16)
        keys_slot = keys.reshape(n_slot, group, head_cols)
        values_slot = values.reshape(n_slot, group, head_cols)
        key_parts = []
        value_parts = []
        for back in range(reach, 0, -1):
            got_keys, got_values = shifted((keys_slot, values_slot), "ctx", back)
            key_parts.append(got_keys)
            value_parts.append(got_values)
        keys_ext = jnp.concatenate(key_parts + [keys_slot], axis=1).reshape(
            n_slot, extent, local_heads, HEAD_DIM
        )
        values_ext = jnp.concatenate(value_parts + [values_slot], axis=1).reshape(
            n_slot, extent, local_heads, HEAD_DIM
        )
        queries_four = queries.reshape(n_slot, group, local_heads, HEAD_DIM)
        scores = scores_of(queries_four, keys_ext, allowed)
        top = jnp.max(scores, axis=-1, keepdims=True)
        expo = jnp.exp(scores - top)
        summed = jnp.sum(expo, axis=-1, keepdims=True)
        logsum = top + jnp.log(summed)
        probs = (expo / summed).astype(jnp.bfloat16)
        attended = jnp.einsum(
            "shqk,skhd->sqhd", probs, values_ext, preferred_element_type=jnp.float32
        )
        attended = attended.astype(jnp.bfloat16).reshape(rows, head_cols)
        branch_a = lax.psum(plain_dot(attended, full_out), "mp")
        mid = x_in + branch_a
        feed_set = fetch_feed()
        full_gate, full_up, full_down, full_gain_f = feed_set
        gain_f = full_gain_f.astype(jnp.float32)
        normed_f = gain_norm(mid, gain_f).astype(jnp.bfloat16)
        gate_val = plain_dot(normed_f, full_gate)
        up_val = plain_dot(normed_f, full_up)
        hidden_units = gated_unit(gate_val, up_val).astype(jnp.bfloat16)
        branch_f = lax.psum(plain_dot(hidden_units, full_down), "mp")
        result = (mid + branch_f) * valid_rows
        target = teacher[micro].reshape(rows, width).astype(jnp.float32)
        error = (result - target) * valid_rows
        loss_part = loss_part + jnp.sum(error * error)
        results.append(result.astype(jnp.bfloat16).reshape(n_slot, group, width))
        back_feed = fetch_feed()
        full_gate, full_up, full_down, full_gain_f = back_feed
        grad_result = error * factor
        grad_branch = grad_result.astype(jnp.bfloat16)
        acc_down = acc_down + left_dot(hidden_units, grad_branch)
        grad_units = right_dot(grad_branch, full_down)
        unused, pull_unit = jax.vjp(gated_unit, gate_val, up_val)
        grad_gate, grad_upper = pull_unit(grad_units)
        grad_gate = grad_gate.astype(jnp.bfloat16)
        grad_upper = grad_upper.astype(jnp.bfloat16)
        acc_gate = acc_gate + left_dot(normed_f, grad_gate)
        acc_up = acc_up + left_dot(normed_f, grad_upper)
        grad_normed_f = lax.psum(
            right_dot(grad_gate, full_gate) + right_dot(grad_upper, full_up), "mp"
        )
        unused, pull_norm = jax.vjp(gain_norm, mid, gain_f)
        grad_mid_norm, grad_gain_f = pull_norm(grad_normed_f)
        acc_gain_f = acc_gain_f + grad_gain_f
        grad_mid = grad_result + grad_mid_norm
        back_attention = fetch_attention()
        full_query, full_key, full_value, full_out, full_gain_a = back_attention
        grad_att = grad_mid.astype(jnp.bfloat16)
        acc_out = acc_out + left_dot(attended, grad_att)
        grad_attended = (
            right_dot(grad_att, full_out)
            .astype(jnp.bfloat16)
            .reshape(n_slot, group, local_heads, HEAD_DIM)
        )
        scores_again = scores_of(queries_four, keys_ext, allowed)
        probs_back = jnp.exp(scores_again - logsum)
        grad_values_ext = jnp.einsum(
            "shqk,sqhd->skhd",
            probs_back.astype(jnp.bfloat16),
            grad_attended,
            preferred_element_type=jnp.float32,
        )
        grad_probs = jnp.einsum(
            "sqhd,skhd->shqk", grad_attended, values_ext, preferred_element_type=jnp.float32
        )
        inner = jnp.sum(probs_back * grad_probs, axis=-1, keepdims=True)
        grad_scores = (probs_back * (grad_probs - inner)).astype(jnp.bfloat16)
        grad_queries = (
            jnp.einsum("shqk,skhd->sqhd", grad_scores, keys_ext, preferred_element_type=jnp.float32)
            * scale
        )
        grad_keys_ext = (
            jnp.einsum(
                "shqk,sqhd->skhd", grad_scores, queries_four, preferred_element_type=jnp.float32
            )
            * scale
        )
        grad_keys_ext = grad_keys_ext.reshape(n_slot, extent, head_cols)
        grad_values_ext = grad_values_ext.reshape(n_slot, extent, head_cols)
        grad_keys_total = grad_keys_ext[:, reach * group :]
        grad_values_total = grad_values_ext[:, reach * group :]
        for back in range(1, reach + 1):
            offset = (reach - back) * group
            piece_keys = grad_keys_ext[:, offset : offset + group]
            piece_values = grad_values_ext[:, offset : offset + group]
            got_keys, got_values = shifted((piece_keys, piece_values), "ctx", -back)
            grad_keys_total = grad_keys_total + got_keys
            grad_values_total = grad_values_total + got_values
        grad_queries = grad_queries.reshape(rows, head_cols).astype(jnp.bfloat16)
        grad_keys_low = grad_keys_total.reshape(rows, head_cols).astype(jnp.bfloat16)
        grad_values_low = grad_values_total.reshape(rows, head_cols).astype(jnp.bfloat16)
        acc_query = acc_query + left_dot(normed_a, grad_queries)
        acc_key = acc_key + left_dot(normed_a, grad_keys_low)
        acc_value = acc_value + left_dot(normed_a, grad_values_low)
        grad_normed_a = (
            right_dot(grad_queries, full_query)
            + right_dot(grad_keys_low, full_key)
            + right_dot(grad_values_low, full_value)
        )
        grad_normed_a = lax.psum(grad_normed_a, "mp")
        unused, pull_first = jax.vjp(gain_norm, x_in, gain_a)
        grad_x_norm, grad_gain_a = pull_first(grad_normed_a)
        acc_gain_a = acc_gain_a + grad_gain_a
        grad_in = grad_mid + grad_x_norm
        input_grads.append(grad_in.astype(jnp.bfloat16).reshape(n_slot, group, width))
    loss = lax.psum(loss_part, ("dp", "ctx")) / (count * width)
    grads = (
        lax.psum_scatter(acc_query, ("dp", "ctx"), scatter_dimension=0, tiled=True),
        lax.psum_scatter(acc_key, ("dp", "ctx"), scatter_dimension=0, tiled=True),
        lax.psum_scatter(acc_value, ("dp", "ctx"), scatter_dimension=0, tiled=True),
        lax.psum_scatter(acc_out, ("dp", "ctx"), scatter_dimension=1, tiled=True),
        lax.psum_scatter(acc_gate, ("dp", "ctx"), scatter_dimension=0, tiled=True),
        lax.psum_scatter(acc_up, ("dp", "ctx"), scatter_dimension=0, tiled=True),
        lax.psum_scatter(acc_down, ("dp", "ctx"), scatter_dimension=1, tiled=True),
        lax.psum_scatter(acc_gain_a, ("dp", "ctx"), scatter_dimension=0, tiled=True),
        lax.psum_scatter(acc_gain_f, ("dp", "ctx"), scatter_dimension=0, tiled=True),
    )
    return (
        jnp.stack(results),
        loss,
        jnp.stack(input_grads),
        grads[0],
        grads[1],
        grads[2],
        grads[3],
        grads[4],
        grads[5],
        grads[6],
        grads[7],
        grads[8],
    )


def solution(mesh):
    in_specs = (
        P(None, "dp", "ctx", None),
        P(None, "dp", "ctx", None),
        P(),
        P(("dp", "ctx"), "mp"),
        P(("dp", "ctx"), "mp"),
        P(("dp", "ctx"), "mp"),
        P("mp", ("dp", "ctx")),
        P(("dp", "ctx"), "mp"),
        P(("dp", "ctx"), "mp"),
        P("mp", ("dp", "ctx")),
        P(("dp", "ctx")),
        P(("dp", "ctx")),
    )
    out_specs = (
        P(None, "dp", "ctx", None),
        P(),
        P(None, "dp", "ctx", None),
        P(("dp", "ctx"), "mp"),
        P(("dp", "ctx"), "mp"),
        P(("dp", "ctx"), "mp"),
        P("mp", ("dp", "ctx")),
        P(("dp", "ctx"), "mp"),
        P(("dp", "ctx"), "mp"),
        P("mp", ("dp", "ctx")),
        P(("dp", "ctx")),
        P(("dp", "ctx")),
    )
    slots = 8 // mesh.shape["dp"]
    whole_slots = mesh.shape["ctx"] == slots and mesh.shape["mp"] == 4
    return jax.shard_map(
        slot_device if whole_slots else on_device, mesh=mesh, in_specs=in_specs, out_specs=out_specs, check_vma=False
    )
```

```python
import jax
import jax.numpy as jnp
from jax import lax
from jax.experimental import pallas as pl
from jax.experimental.pallas import tpu as pltpu
from jax.sharding import PartitionSpec as P

HEAD_DIM = 128
WINDOW = 1024
SEQ = 2048
EPS = 1e-06
NEGATIVE = -1e30
BF = jnp.bfloat16
F32 = jnp.float32


def dot_t(a, b, dims):
    return lax.dot_general(a, b, (dims, ((), ())), preferred_element_type=F32)


def plain_dot(left, right):
    return dot_t(left, right, ((1,), (0,)))


def left_dot(left, right):
    return dot_t(left, right, ((0,), (0,)))


def right_dot(left, right):
    return dot_t(left, right, ((1,), (1,)))


def masked_scores(q, k, behind, length, kcol, qrow, kbase):
    s = right_dot(k, q) * (HEAD_DIM**-0.5)
    valid = kcol + kbase < length
    if behind == 0:
        keep = (qrow >= jnp.where(valid, kcol, SEQ)) | (qrow == kcol)
    elif behind == 1:
        keep = jnp.broadcast_to(valid, s.shape)
    else:
        keep = qrow < jnp.where(valid, kcol, -1)
    return jnp.where(keep, s, NEGATIVE)


def piece(ref, block, rows):
    return ref[block * rows : (block + 1) * rows, :]


def attend_kernel(pair, per, back, len_ref, kcol_ref, qrow_ref, q_ref, *refs):
    n = (len(refs) - 2) // 2
    k_refs, v_refs, (o_ref, lse_ref) = refs[:n], refs[n : 2 * n], refs[2 * n :]
    rows = kcol_ref.shape[0]
    length = len_ref[0]
    kcol, qrow = kcol_ref[...], qrow_ref[...]
    base = (pair - n + 1) * per
    for b in range(per):
        chunk = pair * per + b
        seen = range(max(0, chunk - back), chunk + 1)
        where = [divmod(j - base, per) for j in seen]
        q = piece(q_ref, b, rows)
        scores = [
            masked_scores(q, piece(k_refs[p], i, rows), chunk - j, length, kcol, qrow, j * rows)
            for j, (p, i) in zip(seen, where)
        ]
        top = jnp.max(scores[0], axis=0, keepdims=True)
        for s in scores[1:]:
            top = jnp.maximum(top, jnp.max(s, axis=0, keepdims=True))
        expo = [jnp.exp(s - top) for s in scores]
        total = jnp.sum(expo[0], axis=0, keepdims=True)
        for e in expo[1:]:
            total = total + jnp.sum(e, axis=0, keepdims=True)
        inv = 1.0 / total
        out = jnp.zeros((HEAD_DIM, rows), F32)
        for e, (p, i) in zip(expo, where):
            out = out + left_dot(piece(v_refs[p], i, rows), (e * inv).astype(BF))
        o_ref[b * rows : (b + 1) * rows, :] = out.T.astype(BF)
        lse_ref[0, b : b + 1, :] = top + jnp.log(total)


def attend_back_kernel(pair, per, back, len_ref, kcol_ref, qrow_ref, q_ref, g_ref, lse_ref, *refs):
    n = (len(refs) - 1 + 2) // 6
    k_refs, v_refs = refs[:n], refs[n : 2 * n]
    in_refs = refs[2 * n : 4 * n - 2]
    gq_ref, out_refs = refs[4 * n - 2], refs[4 * n - 1 :]
    rows = kcol_ref.shape[0]
    length = len_ref[0]
    kcol, qrow = kcol_ref[...], qrow_ref[...]
    scale = HEAD_DIM**-0.5
    base = (pair - n + 1) * per
    sums = {}
    for b in range(per):
        chunk = pair * per + b
        seen = range(max(0, chunk - back), chunk + 1)
        where = [divmod(j - base, per) for j in seen]
        q, g = piece(q_ref, b, rows), piece(g_ref, b, rows)
        lse = lse_ref[0, b : b + 1, :]
        probs, gprobs = [], []
        inner = jnp.zeros((1, rows), F32)
        for j, (p, i) in zip(seen, where):
            s = masked_scores(q, piece(k_refs[p], i, rows), chunk - j, length, kcol, qrow, j * rows)
            e = jnp.exp(s - lse)
            ge = right_dot(piece(v_refs[p], i, rows), g)
            inner = inner + jnp.sum(e * ge, axis=0, keepdims=True)
            probs.append(e)
            gprobs.append(ge)
        gq = jnp.zeros((HEAD_DIM, rows), F32)
        for e, ge, at in zip(probs, gprobs, where):
            gs = (e * (ge - inner)).astype(BF)
            gq = gq + left_dot(piece(k_refs[at[0]], at[1], rows), gs)
            gk, gv = plain_dot(gs, q) * scale, plain_dot(e.astype(BF), g)
            if at in sums:
                gk, gv = gk + sums[at][0], gv + sums[at][1]
            sums[at] = (gk, gv)
        gq_ref[b * rows : (b + 1) * rows, :] = (gq.T * scale).astype(BF)
    for p in range(n):
        for i in range(per):
            at = slice(i * rows, (i + 1) * rows)
            for which in range(2):
                out_ref = out_refs[which * n + p]
                value = sums[p, i][which] if (p, i) in sums else None
                if p < n - 1:
                    before = in_refs[which * (n - 1) + p][at, :]
                    value = before if value is None else value + before
                out_ref[at, :] = value.astype(out_ref.dtype)


def attend_call(kernel, name, pair, per, back, kcol, qrow, length, ins, lses, shapes, n_dots):
    rows = kcol.shape[0]
    wide, cols = ins[0].shape
    heads = cols // HEAD_DIM
    block = pl.BlockSpec((wide, HEAD_DIM), lambda h, *_: (0, h))
    lse_block = pl.BlockSpec((1, per, rows), lambda h, *_: (h, 0, 0))
    blocks = sum(min(pair * per + b, back) + 1 for b in range(per))
    n_lse = len(lses)
    return pl.pallas_call(
        lambda *refs: kernel(pair, per, back, *refs),
        grid_spec=pltpu.PrefetchScalarGridSpec(
            num_scalar_prefetch=1,
            grid=(heads,),
            in_specs=[
                pl.BlockSpec((rows, 1), lambda h, *_: (0, 0)),
                pl.BlockSpec((1, rows), lambda h, *_: (0, 0)),
            ]
            + ([block] * 2 + [lse_block] + [block] * (len(ins) - 2) if lses else [block] * len(ins)),
            out_specs=[block if shape.ndim == 2 else lse_block for shape in shapes],
        ),
        out_shape=shapes,
        compiler_params=pltpu.CompilerParams(vmem_limit_bytes=56 << 20),
        cost_estimate=pl.CostEstimate(
            flops=n_dots * blocks * rows * rows * HEAD_DIM * heads,
            bytes_accessed=1 << 16 if lses else 2 * wide * cols * (len(ins) + len(shapes)),
            transcendentals=0 if lses else blocks * rows * rows * heads,
        ),
        name=f"{name}{pair}",
    )(length, kcol, qrow, *((*ins[:2], *lses, *ins[2:]) if lses else ins))


def core_swap(v):
    return lax.ppermute(v, "mp", [(i, i ^ 1) for i in range(4)])


def chip_swap(v):
    return lax.ppermute(v, "mp", [(i, i ^ 2) for i in range(4)])


def dp_swap(v):
    return lax.ppermute(v, "dp", [(i, i ^ 1) for i in range(2)])


def ctx_turn(v, steps):
    n = lax.axis_size("ctx")
    return lax.ppermute(v, "ctx", [(i, (i + steps) % n) for i in range(n)])


def after(value, *others):
    return lax.optimization_barrier((value, *others))[0]


def pick(v, index):
    return lax.dynamic_index_in_dim(v, index, 0, keepdims=False)


def join(got, own):
    return jnp.concatenate([own, got], axis=1)


def join_flat(got, own):
    return join(got, own).reshape(-1, own.shape[2])


class Order:
    def __init__(self):
        self.last = ()

    def __call__(self, step, first, *rest):
        if self.last:
            first = after(first, *self.last)
        out = step(first, *rest)
        self.last = (jax.tree.leaves(out)[0],)
        return out

    def wait(self, *values):
        self.last = (*self.last, *values)


def split_part(part, per):
    part = part.reshape(per, -1, part.shape[1])
    return part[:, part.shape[1] // 2 :].astype(BF), part


def add_core(got, keep):
    mine = keep[:, : keep.shape[1] // 2] + got.astype(F32)
    half = mine.shape[1] // 2
    return mine[:, half:].astype(BF), mine[:, :half]


def own_first(v, y):
    half = v.shape[-1] // 2
    return jnp.where(y == 0, v, jnp.concatenate([v[..., half:], v[..., :half]], axis=-1))


def whole_part(right, left):
    return left_dot(left, right)


def whole_rest(right, left, part):
    return (part + left_dot(left, right)).astype(BF)


def their_part(right, left):
    return left_dot(left[:, left.shape[1] // 2 :], right)


def their_rest(right, left, part):
    return (part + their_part(right, left)).astype(BF)


def own_part_grad(right, left):
    return left_dot(left[:, : left.shape[1] // 2], right)


def own_rest(right, left, part, got):
    return (part + own_part_grad(right, left) + got.astype(F32)).astype(BF)


def both_scatter(grad):
    half = grad.shape[0] // 2
    swapped = jnp.concatenate([grad[half:], grad[:half]], axis=0)
    grad = jnp.where(lax.axis_index("dp") == 0, grad, swapped)
    return lax.psum_scatter(grad, ("dp", "ctx"), scatter_dimension=0, tiled=True)


def to_slots(v, z):
    n = v.shape[0]
    return [pick(v, z)] + [ctx_turn(pick(v, (z + k) % n), k) for k in range(1, n)]


def place_kernel(index_ref, *refs):
    step = pl.program_id(0)
    for i, ref in enumerate(refs[:-1]):

        @pl.when(step == i)
        def _(ref=ref):
            refs[-1][0, 0] = ref[...]


def whole_rows(blocks, index, n):
    rows, width = blocks[0].shape
    return pl.pallas_call(
        place_kernel,
        grid_spec=pltpu.PrefetchScalarGridSpec(
            num_scalar_prefetch=1,
            grid=(len(blocks),),
            in_specs=[
                pl.BlockSpec((rows, width), lambda i, _: (0, 0), pipeline_mode=pl.Buffered(1))
            ]
            * len(blocks),
            out_specs=pl.BlockSpec((1, 1, rows, width), lambda i, at: (at[i, 0], at[i, 1], 0, 0)),
        ),
        out_shape=jax.ShapeDtypeStruct((n, 4, rows, width), blocks[0].dtype),
        compiler_params=pltpu.CompilerParams(vmem_limit_bytes=24 << 20),
        cost_estimate=pl.CostEstimate(
            flops=0, bytes_accessed=4 * len(blocks) * rows * width, transcendentals=0
        ),
        name="place_rows",
    )(jnp.stack([jnp.stack(at) for at in index]).astype(jnp.int32), *blocks)


def all_sum(v):
    v = v + core_swap(v)
    v = v + chip_swap(v)
    v = v + dp_swap(v)
    n = lax.axis_size("ctx")
    step = 1
    while step < n:
        v = v + lax.ppermute(v, "ctx", [(i, i ^ step) for i in range(n)])
        step *= 2
    return v


def norm_scale(v):
    return lax.rsqrt(jnp.mean(v * v, axis=-1, keepdims=True) + EPS)


def norm_back(v, r, gain, grad):
    z = v * r
    e = grad * gain
    return r * (e - z * jnp.mean(e * z, axis=-1, keepdims=True)), jnp.sum(grad * z, axis=(0, 1))


def slot_device(
    hidden_in,
    teacher,
    lengths,
    query_weight,
    key_weight,
    value_weight,
    out_weight,
    gate_weight,
    up_weight,
    down_weight,
    attention_gain,
    feed_gain,
):
    n_micro, n_slot, group, width = hidden_in.shape
    n_chunk = n_micro * n_slot
    quarter = group // 4
    cols = query_weight.shape[1]
    heads = cols // HEAD_DIM
    back = WINDOW // group
    ctx_index = lax.axis_index("ctx")
    dp_index = lax.axis_index("dp")
    mp_index = lax.axis_index("mp")
    core_index, x_index = mp_index % 2, mp_index // 2
    place = core_index * 2 + x_index
    share = attention_gain.shape[0]
    count = jnp.sum(lengths).astype(F32)
    factor = lengths.shape[0] * lengths.shape[1] * SEQ / count
    length = lax.dynamic_slice(
        lengths, (ctx_index // n_slot, dp_index * n_slot + ctx_index % n_slot), (1, 1)
    ).reshape(1)
    row = jnp.arange(group, dtype=jnp.int32)
    inside = ((row // quarter) ^ place) * quarter + row % quarter
    kcol, qrow = inside[:, None], inside[None, :]
    own_inside = place * quarter + jnp.arange(quarter, dtype=jnp.int32)
    chunks = range(n_chunk)

    def own_part(v):
        v = lax.dynamic_slice_in_dim(v.reshape(n_chunk, group, width), place * quarter, quarter, 1)
        return to_slots(own_first(v, dp_index), ctx_index)

    def by_chunk(parts):
        parts = jnp.stack(parts)
        return [pick(parts, (ctx_index - c) % n_chunk) for c in chunks]

    x_parts = own_part(hidden_in)
    x_peers = [chip_swap(part) for part in x_parts]
    x_pairs = [jnp.concatenate(pair, axis=0) for pair in zip(x_parts, x_peers)]
    x_cores = [core_swap(pair) for pair in x_pairs]
    x_own = by_chunk(x_parts)
    x_all = by_chunk([jnp.concatenate(pair, axis=0) for pair in zip(x_pairs, x_cores)])
    gain_rows = jnp.pad(jnp.stack([attention_gain, feed_gain]), ((0, 14), (0, cols - share)))
    shards = [
        jnp.concatenate([query_weight, gain_rows], axis=0),
        key_weight,
        value_weight,
        out_weight.T,
        gate_weight,
        up_weight,
    ]
    parts = []
    for i, shard in enumerate(shards):
        if i > 0:
            shard = after(shard, *x_parts, *parts[-2:-1])
        parts.append(lax.all_gather(shard, "ctx", axis=0, tiled=True))
    shard = after(down_weight.T, *x_parts, *parts[-2:-1])
    part_down = [
        lax.all_gather(v, "ctx", axis=0, tiled=True) for v in (shard, dp_swap(down_weight.T))
    ]
    w_down = jnp.concatenate(part_down, axis=0)
    gates = [x_parts, x_peers, x_cores] + [()] * 3
    fetched = [(part, dp_swap(after(part, *gate))) for part, gate in zip(parts, gates)]
    query_parts = [part.reshape(n_chunk, share + 16, cols) for part in fetched[0]]
    fetched[0] = [part[:, :share].reshape(n_chunk * share, cols) for part in query_parts]
    gain_a, gain_f = [
        jnp.concatenate([part[:, share + i, :share].reshape(-1) for part in query_parts]).astype(F32)
        for i in range(2)
    ]
    part_gate, part_up = parts[4:]
    w_query, w_key, w_value, w_out, w_gate, w_up = [
        jnp.concatenate(pair, axis=0) for pair in fetched
    ]
    teacher_parts = own_part(after(teacher, part_down[1]))
    target = by_chunk(teacher_parts)
    per = 2
    pairs = range(n_chunk // per)
    x_own = [jnp.stack(x_own[p * per : (p + 1) * per]) for p in pairs]
    target = [jnp.stack(target[p * per : (p + 1) * per]) for p in pairs]
    order = Order()
    reach = -(-back // per)
    mid, r_f, sent, kept = [], [], {}, {}

    def gather_half(own):
        return order(join, chip_swap(own), own)

    def gather_rest(pair):
        return order(join_flat, core_swap(pair), pair)

    def pass_core(p):
        sent[p], kept[p] = order(add_core, core_swap(sent[p]), kept[p])

    h1, queries, keys, values, attended, lse, h2 = [], [], [], [], [], [], []

    def project(h):
        return [plain_dot(h, w).astype(BF) for w in (w_query, w_key, w_value)]

    def normed(*xs):
        x = jnp.concatenate(xs, axis=0).astype(F32)
        return (x * norm_scale(x) * gain_a).astype(BF)

    def attention(p):
        first = max(0, p - reach)

        def step(q):
            ins = [q, *keys[first : p + 1], *values[first : p + 1]]
            shapes = [
                jax.ShapeDtypeStruct(q.shape, BF),
                jax.ShapeDtypeStruct((heads, per, group), F32),
            ]
            return attend_call(
                attend_kernel, "attend", p, per, back, kcol, qrow, length, ins, [], shapes, 24
            )

        a, l = order(step, queries[p])
        attended.append(a)
        lse.append(l)

    def enter_feed(p):
        def step(got, keep, x):
            v = x.astype(F32) + (keep + got.astype(F32))
            r = norm_scale(v)
            return (v * r * gain_f).astype(BF), v, r

        low, v, r = order(step, chip_swap(sent[p]), kept[p], x_own[p])
        mid.append(v)
        r_f.append(r)
        return low

    for p in pairs:
        h1.append(order(normed, *x_all[p * per : (p + 1) * per]))
    for p in pairs:
        q, k, v = order(project, h1[p])
        queries.append(q)
        keys.append(k)
        values.append(v)
        order.wait((parts[3], part_gate)[p])
        attention(p)
        sent[p], kept[p] = order(lambda a: split_part(right_dot(a, w_out), per), attended[p])
    pass_core(0)
    order.wait(fetched[4][1])
    pass_core(1)
    low = [enter_feed(0)]
    order.wait(part_up)
    low.append(enter_feed(1))
    low = [gather_half(v) for v in low]
    order.wait(fetched[5][1])
    h2.append(gather_rest(low[0]))

    gate, up, hidden, results, g_result, g_branch, loss_parts = [], [], [], [], [], [], []

    def unit(h):
        g, u = plain_dot(h, w_gate), plain_dot(h, w_up)
        return (g * jax.nn.sigmoid(g) * u).astype(BF), g, u

    def finish(p):
        def step(got, keep, v, t):
            at = (p * per + jnp.arange(per, dtype=jnp.int32))[:, None] * group + own_inside
            valid = (at < length)[:, :, None].astype(F32)
            result = (v + (keep + got.astype(F32))) * valid
            error = (result - t.astype(F32)) * valid
            grad = error * factor
            return grad.astype(BF), grad, result.astype(BF), jnp.sum(error * error)

        low, grad, result, loss = order(step, chip_swap(sent[p]), kept[p], mid[p], target[p])
        results.append(result)
        g_result.append(grad)
        loss_parts.append(loss)
        return low

    def feed(p):
        h, g, u = order(unit, h2[p])
        hidden.append(h)
        gate.append(g)
        up.append(u)

    def project_down(p):
        sent[p], kept[p] = order(lambda h: split_part(right_dot(h, w_down), per), hidden[p])

    g_gate, g_up, g_mid, g_att, gain_f_parts = [], [], [], [], []

    def leave_unit(p):
        def step(g_out, g, u):
            g_hidden = plain_dot(g_out, w_down)
            sig = jax.nn.sigmoid(g)
            return (
                (g_hidden * g * sig).astype(BF),
                (g_hidden * u * sig * (1.0 + g * (1.0 - sig))).astype(BF),
            )

        gu, gg = order(step, g_branch[p], gate[p], up[p])
        g_up.append(gu)
        g_gate.append(gg)

    def project_unit(p):
        def step(gg, gu):
            return split_part(right_dot(gg, w_gate) + right_dot(gu, w_up), per)

        sent[p], kept[p] = order(step, g_gate[p], g_up[p])

    def enter_attention(p):
        def step(got, keep, v, r, grad):
            g_norm, g_gain = norm_back(v, r, gain_f, keep + got.astype(F32))
            total = grad + g_norm
            return total.astype(BF), total, g_gain

        low, total, g_gain = order(step, chip_swap(sent[p]), kept[p], mid[p], r_f[p], g_result[p])
        g_mid.append(total)
        gain_f_parts.append(g_gain)
        return low

    scattered = []

    def scatter(rights, lefts, got):
        part = order(own_part_grad, rights[0], lefts[0])
        own = order(own_rest, rights[1], lefts[1], part, got)
        scattered.append(lax.psum_scatter(own, "ctx", scatter_dimension=0, tiled=True))

    def send(rights, lefts):
        part = order(their_part, rights[0], lefts[0])
        return dp_swap(order(their_rest, rights[1], lefts[1], part))

    g_q, g_k, g_v = [None] * len(pairs), [None] * len(pairs), [None] * len(pairs)
    g_in, gain_a_parts = [], []

    def attention_back(p):
        first = max(0, p - reach)
        last = p == len(pairs) - 1

        def step(g):
            ins = [queries[p], plain_dot(g, w_out).astype(BF), *keys[first : p + 1], *values[first : p + 1]]
            kinds = [BF if last or p - j == reach else F32 for j in range(first, p + 1)]
            shape = ins[0].shape
            shapes = [jax.ShapeDtypeStruct(shape, kind) for kind in [BF] + kinds * 2]
            return attend_call(
                attend_back_kernel, "attend_back", p, per, back, kcol, qrow, length,
                [*ins, *g_k[first:p], *g_v[first:p]], [lse[p]], shapes, 0,
            )

        out = order(step, g_att[p])
        n = p - first + 1
        g_q[p] = out[0]
        g_k[first : p + 1] = out[1 : 1 + n]
        g_v[first : p + 1] = out[1 + n :]

    def project_back(p):
        def step(q, k, v):
            whole = right_dot(q, w_query) + right_dot(k, w_key) + right_dot(v, w_value)
            return split_part(whole, per)

        sent[p], kept[p] = order(step, g_q[p], g_k[p], g_v[p])

    def leave(p):
        def step(got, keep, x, grad):
            x = x.astype(F32)
            g_norm, g_gain = norm_back(x, norm_scale(x), gain_a, keep + got.astype(F32))
            return (grad + g_norm).astype(BF), g_gain

        low, g_gain = order(step, chip_swap(sent[p]), kept[p], x_own[p], g_mid[p])
        g_in.append(low)
        gain_a_parts.append(g_gain)

    feed(0)
    order.wait(*teacher_parts)
    project_down(0)
    h2.append(gather_rest(low[1]))
    pass_core(0)
    feed(1)
    first = finish(0)
    project_down(1)
    pass_core(1)
    g_branch.append(gather_rest(gather_half(first)))
    leave_unit(0)
    part = order(whole_part, hidden[0], g_branch[0])
    second = finish(1)
    out_parts = to_slots(own_first(jnp.concatenate(results, axis=0), dp_index), ctx_index)
    project_unit(0)
    pass_core(0)
    order.wait(*out_parts)
    g_branch.append(gather_rest(gather_half(second)))
    leave_unit(1)
    s_down = both_scatter(order(whole_rest, hidden[1], g_branch[1], part))
    first = enter_attention(0)
    project_unit(1)
    pass_core(1)
    part = order(whole_part, g_gate[0], h2[0])
    s_gate = both_scatter(order(whole_rest, g_gate[1], h2[1], part))
    g_att.append(gather_rest(gather_half(first)))
    attention_back(0)
    order.wait(s_down)
    second = enter_attention(1)
    g_att.append(gather_rest(gather_half(second)))
    part = order(whole_part, g_up[0], h2[0])
    s_up = both_scatter(order(whole_rest, g_up[1], h2[1], part))
    out_got = send(attended, g_att)
    out_own = order(lambda first, *rest: jnp.stack([first, *rest]), *out_parts)
    out_peer, out_core = chip_swap(out_own), core_swap(out_own)
    attention_back(1)
    order.wait(out_peer, out_got)
    project_back(0)
    pass_core(0)
    rights = [
        order(lambda q, k, v: jnp.concatenate([q, k, v], axis=1), g_q[p], g_k[p], g_v[p]) for p in pairs
    ]
    qkv_got = send(rights, h1)
    order.wait(s_gate)
    project_back(1)
    leave(0)
    pass_core(1)
    leave(1)
    back_parts = to_slots(own_first(jnp.concatenate(g_in, axis=0), dp_index), ctx_index)
    scatter(attended, g_att, out_got)
    part = order(own_part_grad, rights[0], h1[0])
    slots = [(ctx_index - k) % n_chunk for k in chunks]
    index = [(slot, place ^ i) for slot in slots for i in range(4)]

    def place_out(own, *others):
        blocks = [v[k] for k in chunks for v in (own, *others)]
        return whole_rows(blocks, index, n_chunk)

    order.wait(*back_parts, qkv_got)
    out_hidden = order(place_out, out_own, out_peer, out_core, core_swap(out_peer))
    back_peers = [chip_swap(own) for own in back_parts]
    order.wait(s_up, *back_peers)
    own = order(own_rest, rights[1], h1[1], part, qkv_got)
    s_qkv = lax.psum_scatter(own, "ctx", scatter_dimension=0, tiled=True).astype(F32)
    back_blocks = []
    for own, peer in zip(back_parts, back_peers):
        back_blocks += [own, peer, core_swap(own), core_swap(peer)]
    grad_hidden = order(lambda first, *rest: whole_rows([first, *rest], index, n_chunk), *back_blocks)
    grad_down, grad_gate, grad_up = [v.astype(F32) for v in (s_down, s_gate, s_up)]
    gain_a_part, gain_f_part, loss_part = sum(gain_a_parts), sum(gain_f_parts), sum(loss_parts)
    small = jnp.concatenate(
        [own_first(gain_a_part, dp_index), own_first(gain_f_part, dp_index), jnp.full((128,), loss_part)]
    )
    small = all_sum(after(small, *back_peers).reshape(-1, 128)).reshape(-1)
    at = (dp_index * n_chunk + ctx_index) * share
    shape = hidden_in.shape
    return (
        out_hidden.reshape(shape),
        small[2 * width] / (count * width),
        grad_hidden.reshape(shape),
        s_qkv[:, :cols],
        s_qkv[:, cols : 2 * cols],
        s_qkv[:, 2 * cols :],
        scattered[0].astype(F32).T,
        grad_gate,
        grad_up,
        grad_down.T,
        lax.dynamic_slice_in_dim(small, at, share),
        lax.dynamic_slice_in_dim(small, width + at, share),
    )


def shifted(value, axis, steps):
    count = lax.axis_size(axis)
    leading, last = (max(0, -steps), min(count, count - steps))
    return lax.ppermute(value, axis, [(source, source + steps) for source in range(leading, last)])


def norm_rows(v):
    return v * lax.rsqrt(jnp.mean(v * v, axis=-1, keepdims=True) + EPS)


def silu(v):
    return v * jax.nn.sigmoid(v)


def gain_norm(values, gain):
    return norm_rows(values) * gain


def gated_unit(gate, upper):
    return silu(gate) * upper


def on_device(
    hidden_in,
    teacher,
    lengths,
    query_weight,
    key_weight,
    value_weight,
    out_weight,
    gate_weight,
    up_weight,
    down_weight,
    attention_gain,
    feed_gain,
):
    n_micro, n_slot, group, width = hidden_in.shape
    local_heads = query_weight.shape[1] // HEAD_DIM
    head_cols = query_weight.shape[1]
    reach = WINDOW // group
    extent = (reach + 1) * group
    rows = n_slot * group
    scale = HEAD_DIM ** (-0.5)
    ctx_index = lax.axis_index("ctx")
    dp_index = lax.axis_index("dp")
    count = jnp.sum(lengths).astype(jnp.float32)
    factor = lengths.shape[0] * lengths.shape[1] * SEQ / count
    own_lengths = lax.dynamic_slice_in_dim(lengths, dp_index * n_slot, n_slot, 1)
    positions = ctx_index * group + jnp.arange(group, dtype=jnp.int32)
    key_positions = ctx_index * group - reach * group + jnp.arange(extent, dtype=jnp.int32)
    distance = positions[:, None] - key_positions[None, :]
    in_window = (distance >= 0) & (distance < WINDOW) & (key_positions[None, :] >= 0)

    def fetch_attention():
        return (
            lax.all_gather(query_weight, ("dp", "ctx"), axis=0, tiled=True),
            lax.all_gather(key_weight, ("dp", "ctx"), axis=0, tiled=True),
            lax.all_gather(value_weight, ("dp", "ctx"), axis=0, tiled=True),
            lax.all_gather(out_weight, ("dp", "ctx"), axis=1, tiled=True),
            lax.all_gather(attention_gain, ("dp", "ctx"), axis=0, tiled=True),
        )

    def fetch_feed():
        return (
            lax.all_gather(gate_weight, ("dp", "ctx"), axis=0, tiled=True),
            lax.all_gather(up_weight, ("dp", "ctx"), axis=0, tiled=True),
            lax.all_gather(down_weight, ("dp", "ctx"), axis=1, tiled=True),
            lax.all_gather(feed_gain, ("dp", "ctx"), axis=0, tiled=True),
        )

    acc_query = jnp.zeros((width, head_cols), jnp.float32)
    acc_key = jnp.zeros((width, head_cols), jnp.float32)
    acc_value = jnp.zeros((width, head_cols), jnp.float32)
    acc_out = jnp.zeros((head_cols, width), jnp.float32)
    acc_gate = jnp.zeros((width, gate_weight.shape[1]), jnp.float32)
    acc_up = jnp.zeros((width, gate_weight.shape[1]), jnp.float32)
    acc_down = jnp.zeros((gate_weight.shape[1], width), jnp.float32)
    acc_gain_a = jnp.zeros((width,), jnp.float32)
    acc_gain_f = jnp.zeros((width,), jnp.float32)
    loss_part = jnp.zeros((), jnp.float32)
    results = []
    input_grads = []

    def scores_of(queries_four, keys_ext, allowed):
        raw = (
            jnp.einsum(
                "sqhd,skhd->shqk", queries_four, keys_ext, preferred_element_type=jnp.float32
            )
            * scale
        )
        return jnp.where(allowed[:, None], raw, NEGATIVE)

    for micro in range(n_micro):
        slot_len = own_lengths[micro]
        valid = positions[None, :] < slot_len[:, None]
        key_ok = (key_positions[None, None, :] < slot_len[:, None, None]) | (distance == 0)[None]
        allowed = in_window[None] & key_ok
        valid_rows = valid.reshape(rows, 1).astype(jnp.float32)
        attention_set = fetch_attention()
        full_query, full_key, full_value, full_out, full_gain_a = attention_set
        gain_a = full_gain_a.astype(jnp.float32)
        x_in = hidden_in[micro].reshape(rows, width).astype(jnp.float32)
        normed_a = gain_norm(x_in, gain_a).astype(jnp.bfloat16)
        queries = plain_dot(normed_a, full_query).astype(jnp.bfloat16)
        keys = plain_dot(normed_a, full_key).astype(jnp.bfloat16)
        values = plain_dot(normed_a, full_value).astype(jnp.bfloat16)
        keys_slot = keys.reshape(n_slot, group, head_cols)
        values_slot = values.reshape(n_slot, group, head_cols)
        key_parts = []
        value_parts = []
        for back in range(reach, 0, -1):
            got_keys, got_values = shifted((keys_slot, values_slot), "ctx", back)
            key_parts.append(got_keys)
            value_parts.append(got_values)
        keys_ext = jnp.concatenate(key_parts + [keys_slot], axis=1).reshape(
            n_slot, extent, local_heads, HEAD_DIM
        )
        values_ext = jnp.concatenate(value_parts + [values_slot], axis=1).reshape(
            n_slot, extent, local_heads, HEAD_DIM
        )
        queries_four = queries.reshape(n_slot, group, local_heads, HEAD_DIM)
        scores = scores_of(queries_four, keys_ext, allowed)
        top = jnp.max(scores, axis=-1, keepdims=True)
        expo = jnp.exp(scores - top)
        summed = jnp.sum(expo, axis=-1, keepdims=True)
        logsum = top + jnp.log(summed)
        probs = (expo / summed).astype(jnp.bfloat16)
        attended = jnp.einsum(
            "shqk,skhd->sqhd", probs, values_ext, preferred_element_type=jnp.float32
        )
        attended = attended.astype(jnp.bfloat16).reshape(rows, head_cols)
        branch_a = lax.psum(plain_dot(attended, full_out), "mp")
        mid = x_in + branch_a
        feed_set = fetch_feed()
        full_gate, full_up, full_down, full_gain_f = feed_set
        gain_f = full_gain_f.astype(jnp.float32)
        normed_f = gain_norm(mid, gain_f).astype(jnp.bfloat16)
        gate_val = plain_dot(normed_f, full_gate)
        up_val = plain_dot(normed_f, full_up)
        hidden_units = gated_unit(gate_val, up_val).astype(jnp.bfloat16)
        branch_f = lax.psum(plain_dot(hidden_units, full_down), "mp")
        result = (mid + branch_f) * valid_rows
        target = teacher[micro].reshape(rows, width).astype(jnp.float32)
        error = (result - target) * valid_rows
        loss_part = loss_part + jnp.sum(error * error)
        results.append(result.astype(jnp.bfloat16).reshape(n_slot, group, width))
        back_feed = fetch_feed()
        full_gate, full_up, full_down, full_gain_f = back_feed
        grad_result = error * factor
        grad_branch = grad_result.astype(jnp.bfloat16)
        acc_down = acc_down + left_dot(hidden_units, grad_branch)
        grad_units = right_dot(grad_branch, full_down)
        unused, pull_unit = jax.vjp(gated_unit, gate_val, up_val)
        grad_gate, grad_upper = pull_unit(grad_units)
        grad_gate = grad_gate.astype(jnp.bfloat16)
        grad_upper = grad_upper.astype(jnp.bfloat16)
        acc_gate = acc_gate + left_dot(normed_f, grad_gate)
        acc_up = acc_up + left_dot(normed_f, grad_upper)
        grad_normed_f = lax.psum(
            right_dot(grad_gate, full_gate) + right_dot(grad_upper, full_up), "mp"
        )
        unused, pull_norm = jax.vjp(gain_norm, mid, gain_f)
        grad_mid_norm, grad_gain_f = pull_norm(grad_normed_f)
        acc_gain_f = acc_gain_f + grad_gain_f
        grad_mid = grad_result + grad_mid_norm
        back_attention = fetch_attention()
        full_query, full_key, full_value, full_out, full_gain_a = back_attention
        grad_att = grad_mid.astype(jnp.bfloat16)
        acc_out = acc_out + left_dot(attended, grad_att)
        grad_attended = (
            right_dot(grad_att, full_out)
            .astype(jnp.bfloat16)
            .reshape(n_slot, group, local_heads, HEAD_DIM)
        )
        scores_again = scores_of(queries_four, keys_ext, allowed)
        probs_back = jnp.exp(scores_again - logsum)
        grad_values_ext = jnp.einsum(
            "shqk,sqhd->skhd",
            probs_back.astype(jnp.bfloat16),
            grad_attended,
            preferred_element_type=jnp.float32,
        )
        grad_probs = jnp.einsum(
            "sqhd,skhd->shqk", grad_attended, values_ext, preferred_element_type=jnp.float32
        )
        inner = jnp.sum(probs_back * grad_probs, axis=-1, keepdims=True)
        grad_scores = (probs_back * (grad_probs - inner)).astype(jnp.bfloat16)
        grad_queries = (
            jnp.einsum("shqk,skhd->sqhd", grad_scores, keys_ext, preferred_element_type=jnp.float32)
            * scale
        )
        grad_keys_ext = (
            jnp.einsum(
                "shqk,sqhd->skhd", grad_scores, queries_four, preferred_element_type=jnp.float32
            )
            * scale
        )
        grad_keys_ext = grad_keys_ext.reshape(n_slot, extent, head_cols)
        grad_values_ext = grad_values_ext.reshape(n_slot, extent, head_cols)
        grad_keys_total = grad_keys_ext[:, reach * group :]
        grad_values_total = grad_values_ext[:, reach * group :]
        for back in range(1, reach + 1):
            offset = (reach - back) * group
            piece_keys = grad_keys_ext[:, offset : offset + group]
            piece_values = grad_values_ext[:, offset : offset + group]
            got_keys, got_values = shifted((piece_keys, piece_values), "ctx", -back)
            grad_keys_total = grad_keys_total + got_keys
            grad_values_total = grad_values_total + got_values
        grad_queries = grad_queries.reshape(rows, head_cols).astype(jnp.bfloat16)
        grad_keys_low = grad_keys_total.reshape(rows, head_cols).astype(jnp.bfloat16)
        grad_values_low = grad_values_total.reshape(rows, head_cols).astype(jnp.bfloat16)
        acc_query = acc_query + left_dot(normed_a, grad_queries)
        acc_key = acc_key + left_dot(normed_a, grad_keys_low)
        acc_value = acc_value + left_dot(normed_a, grad_values_low)
        grad_normed_a = (
            right_dot(grad_queries, full_query)
            + right_dot(grad_keys_low, full_key)
            + right_dot(grad_values_low, full_value)
        )
        grad_normed_a = lax.psum(grad_normed_a, "mp")
        unused, pull_first = jax.vjp(gain_norm, x_in, gain_a)
        grad_x_norm, grad_gain_a = pull_first(grad_normed_a)
        acc_gain_a = acc_gain_a + grad_gain_a
        grad_in = grad_mid + grad_x_norm
        input_grads.append(grad_in.astype(jnp.bfloat16).reshape(n_slot, group, width))
    loss = lax.psum(loss_part, ("dp", "ctx")) / (count * width)
    grads = (
        lax.psum_scatter(acc_query, ("dp", "ctx"), scatter_dimension=0, tiled=True),
        lax.psum_scatter(acc_key, ("dp", "ctx"), scatter_dimension=0, tiled=True),
        lax.psum_scatter(acc_value, ("dp", "ctx"), scatter_dimension=0, tiled=True),
        lax.psum_scatter(acc_out, ("dp", "ctx"), scatter_dimension=1, tiled=True),
        lax.psum_scatter(acc_gate, ("dp", "ctx"), scatter_dimension=0, tiled=True),
        lax.psum_scatter(acc_up, ("dp", "ctx"), scatter_dimension=0, tiled=True),
        lax.psum_scatter(acc_down, ("dp", "ctx"), scatter_dimension=1, tiled=True),
        lax.psum_scatter(acc_gain_a, ("dp", "ctx"), scatter_dimension=0, tiled=True),
        lax.psum_scatter(acc_gain_f, ("dp", "ctx"), scatter_dimension=0, tiled=True),
    )
    return (
        jnp.stack(results),
        loss,
        jnp.stack(input_grads),
        grads[0],
        grads[1],
        grads[2],
        grads[3],
        grads[4],
        grads[5],
        grads[6],
        grads[7],
        grads[8],
    )


def solution(mesh):
    in_specs = (
        P(None, "dp", "ctx", None),
        P(None, "dp", "ctx", None),
        P(),
        P(("dp", "ctx"), "mp"),
        P(("dp", "ctx"), "mp"),
        P(("dp", "ctx"), "mp"),
        P("mp", ("dp", "ctx")),
        P(("dp", "ctx"), "mp"),
        P(("dp", "ctx"), "mp"),
        P("mp", ("dp", "ctx")),
        P(("dp", "ctx")),
        P(("dp", "ctx")),
    )
    out_specs = (
        P(None, "dp", "ctx", None),
        P(),
        P(None, "dp", "ctx", None),
        P(("dp", "ctx"), "mp"),
        P(("dp", "ctx"), "mp"),
        P(("dp", "ctx"), "mp"),
        P("mp", ("dp", "ctx")),
        P(("dp", "ctx"), "mp"),
        P(("dp", "ctx"), "mp"),
        P("mp", ("dp", "ctx")),
        P(("dp", "ctx")),
        P(("dp", "ctx")),
    )
    slots = 8 // mesh.shape["dp"]
    whole_slots = mesh.shape["ctx"] == slots and mesh.shape["mp"] == 4
    return jax.shard_map(
        slot_device if whole_slots else on_device, mesh=mesh, in_specs=in_specs, out_specs=out_specs, check_vma=False
    )
```

```python
import jax
import jax.numpy as jnp
from jax import lax
from jax.experimental import pallas as pl
from jax.experimental.pallas import tpu as pltpu
from jax.sharding import PartitionSpec as P

HEAD_DIM = 128
WINDOW = 1024
SEQ = 2048
EPS = 1e-06
NEGATIVE = -1e30
BF = jnp.bfloat16
F32 = jnp.float32


def dot_t(a, b, dims):
    return lax.dot_general(a, b, (dims, ((), ())), preferred_element_type=F32)


def plain_dot(left, right):
    return dot_t(left, right, ((1,), (0,)))


def left_dot(left, right):
    return dot_t(left, right, ((0,), (0,)))


def right_dot(left, right):
    return dot_t(left, right, ((1,), (1,)))


def masked_scores(q, k, behind, length, kcol, qrow, kbase):
    s = right_dot(k, q) * (HEAD_DIM**-0.5)
    valid = kcol + kbase < length
    if behind == 0:
        keep = (qrow >= jnp.where(valid, kcol, SEQ)) | (qrow == kcol)
    elif behind == 1:
        keep = jnp.broadcast_to(valid, s.shape)
    else:
        keep = qrow < jnp.where(valid, kcol, -1)
    return jnp.where(keep, s, NEGATIVE)


def piece(ref, block, rows):
    return ref[block * rows : (block + 1) * rows, :]


def attend_kernel(pair, per, back, len_ref, kcol_ref, qrow_ref, q_ref, *refs):
    n = (len(refs) - 2) // 2
    k_refs, v_refs, (o_ref, lse_ref) = refs[:n], refs[n : 2 * n], refs[2 * n :]
    rows = kcol_ref.shape[0]
    length = len_ref[0]
    kcol, qrow = kcol_ref[...], qrow_ref[...]
    base = (pair - n + 1) * per
    for b in range(per):
        chunk = pair * per + b
        seen = range(max(0, chunk - back), chunk + 1)
        where = [divmod(j - base, per) for j in seen]
        q = piece(q_ref, b, rows)
        scores = [
            masked_scores(q, piece(k_refs[p], i, rows), chunk - j, length, kcol, qrow, j * rows)
            for j, (p, i) in zip(seen, where)
        ]
        top = jnp.max(scores[0], axis=0, keepdims=True)
        for s in scores[1:]:
            top = jnp.maximum(top, jnp.max(s, axis=0, keepdims=True))
        expo = [jnp.exp(s - top) for s in scores]
        total = jnp.sum(expo[0], axis=0, keepdims=True)
        for e in expo[1:]:
            total = total + jnp.sum(e, axis=0, keepdims=True)
        inv = 1.0 / total
        out = jnp.zeros((HEAD_DIM, rows), F32)
        for e, (p, i) in zip(expo, where):
            out = out + left_dot(piece(v_refs[p], i, rows), (e * inv).astype(BF))
        o_ref[b * rows : (b + 1) * rows, :] = out.T.astype(BF)
        lse_ref[0, b : b + 1, :] = top + jnp.log(total)


def attend_back_kernel(pair, per, back, len_ref, kcol_ref, qrow_ref, q_ref, g_ref, lse_ref, *refs):
    n = (len(refs) - 1 + 2) // 6
    k_refs, v_refs = refs[:n], refs[n : 2 * n]
    in_refs = refs[2 * n : 4 * n - 2]
    gq_ref, out_refs = refs[4 * n - 2], refs[4 * n - 1 :]
    rows = kcol_ref.shape[0]
    length = len_ref[0]
    kcol, qrow = kcol_ref[...], qrow_ref[...]
    scale = HEAD_DIM**-0.5
    base = (pair - n + 1) * per
    sums = {}
    for b in range(per):
        chunk = pair * per + b
        seen = range(max(0, chunk - back), chunk + 1)
        where = [divmod(j - base, per) for j in seen]
        q, g = piece(q_ref, b, rows), piece(g_ref, b, rows)
        lse = lse_ref[0, b : b + 1, :]
        probs, gprobs = [], []
        inner = jnp.zeros((1, rows), F32)
        for j, (p, i) in zip(seen, where):
            s = masked_scores(q, piece(k_refs[p], i, rows), chunk - j, length, kcol, qrow, j * rows)
            e = jnp.exp(s - lse)
            ge = right_dot(piece(v_refs[p], i, rows), g)
            inner = inner + jnp.sum(e * ge, axis=0, keepdims=True)
            probs.append(e)
            gprobs.append(ge)
        gq = jnp.zeros((HEAD_DIM, rows), F32)
        for e, ge, at in zip(probs, gprobs, where):
            gs = (e * (ge - inner)).astype(BF)
            gq = gq + left_dot(piece(k_refs[at[0]], at[1], rows), gs)
            gk, gv = plain_dot(gs, q) * scale, plain_dot(e.astype(BF), g)
            if at in sums:
                gk, gv = gk + sums[at][0], gv + sums[at][1]
            sums[at] = (gk, gv)
        gq_ref[b * rows : (b + 1) * rows, :] = (gq.T * scale).astype(BF)
    for p in range(n):
        for i in range(per):
            at = slice(i * rows, (i + 1) * rows)
            for which in range(2):
                out_ref = out_refs[which * n + p]
                value = sums[p, i][which] if (p, i) in sums else None
                if p < n - 1:
                    before = in_refs[which * (n - 1) + p][at, :]
                    value = before if value is None else value + before
                out_ref[at, :] = value.astype(out_ref.dtype)


def attend_call(kernel, name, pair, per, back, kcol, qrow, length, ins, lses, shapes, n_dots):
    rows = kcol.shape[0]
    wide, cols = ins[0].shape
    heads = cols // HEAD_DIM
    block = pl.BlockSpec((wide, HEAD_DIM), lambda h, *_: (0, h))
    lse_block = pl.BlockSpec((1, per, rows), lambda h, *_: (h, 0, 0))
    blocks = sum(min(pair * per + b, back) + 1 for b in range(per))
    n_lse = len(lses)
    return pl.pallas_call(
        lambda *refs: kernel(pair, per, back, *refs),
        grid_spec=pltpu.PrefetchScalarGridSpec(
            num_scalar_prefetch=1,
            grid=(heads,),
            in_specs=[
                pl.BlockSpec((rows, 1), lambda h, *_: (0, 0)),
                pl.BlockSpec((1, rows), lambda h, *_: (0, 0)),
            ]
            + ([block] * 2 + [lse_block] + [block] * (len(ins) - 2) if lses else [block] * len(ins)),
            out_specs=[block if shape.ndim == 2 else lse_block for shape in shapes],
        ),
        out_shape=shapes,
        compiler_params=pltpu.CompilerParams(vmem_limit_bytes=56 << 20),
        cost_estimate=pl.CostEstimate(
            flops=n_dots * blocks * rows * rows * HEAD_DIM * heads,
            bytes_accessed=1 << 16 if lses else 2 * wide * cols * (len(ins) + len(shapes)),
            transcendentals=0 if lses else blocks * rows * rows * heads,
        ),
        name=f"{name}{pair}",
    )(length, kcol, qrow, *((*ins[:2], *lses, *ins[2:]) if lses else ins))


def core_swap(v):
    return lax.ppermute(v, "mp", [(i, i ^ 1) for i in range(4)])


def chip_swap(v):
    return lax.ppermute(v, "mp", [(i, i ^ 2) for i in range(4)])


def dp_swap(v):
    return lax.ppermute(v, "dp", [(i, i ^ 1) for i in range(2)])


def ctx_turn(v, steps):
    n = lax.axis_size("ctx")
    return lax.ppermute(v, "ctx", [(i, (i + steps) % n) for i in range(n)])


def after(value, *others):
    return lax.optimization_barrier((value, *others))[0]


def pick(v, index):
    return lax.dynamic_index_in_dim(v, index, 0, keepdims=False)


def join(got, own):
    return jnp.concatenate([own, got], axis=1)


def join_flat(got, own):
    return join(got, own).reshape(-1, own.shape[2])


class Order:
    def __init__(self):
        self.last = ()

    def __call__(self, step, first, *rest):
        if self.last:
            first = after(first, *self.last)
        out = step(first, *rest)
        self.last = (jax.tree.leaves(out)[0],)
        return out

    def wait(self, *values):
        self.last = (*self.last, *values)


def split_part(part, per):
    part = part.reshape(per, -1, part.shape[1])
    return part[:, part.shape[1] // 2 :].astype(BF), part


def add_core(got, keep):
    mine = keep[:, : keep.shape[1] // 2] + got.astype(F32)
    half = mine.shape[1] // 2
    return mine[:, half:].astype(BF), mine[:, :half]


def own_first(v, y):
    half = v.shape[-1] // 2
    return jnp.where(y == 0, v, jnp.concatenate([v[..., half:], v[..., :half]], axis=-1))


def whole_part(right, left):
    return left_dot(left, right)


def whole_rest(right, left, part):
    return (part + left_dot(left, right)).astype(BF)


def their_part(right, left):
    return left_dot(left[:, left.shape[1] // 2 :], right)


def their_rest(right, left, part):
    return (part + their_part(right, left)).astype(BF)


def own_part_grad(right, left):
    return left_dot(left[:, : left.shape[1] // 2], right)


def own_rest(right, left, part, got):
    return (part + own_part_grad(right, left) + got.astype(F32)).astype(BF)


def both_scatter(grad):
    half = grad.shape[0] // 2
    swapped = jnp.concatenate([grad[half:], grad[:half]], axis=0)
    grad = jnp.where(lax.axis_index("dp") == 0, grad, swapped)
    return lax.psum_scatter(grad, ("dp", "ctx"), scatter_dimension=0, tiled=True)


def to_slots(v, z):
    n = v.shape[0]
    return [pick(v, z)] + [ctx_turn(pick(v, (z + k) % n), k) for k in range(1, n)]


def place_kernel(index_ref, *refs):
    step = pl.program_id(0)
    for i, ref in enumerate(refs[:-1]):

        @pl.when(step == i)
        def _(ref=ref):
            refs[-1][0, 0] = ref[...]


def whole_rows(blocks, index, n):
    rows, width = blocks[0].shape
    return pl.pallas_call(
        place_kernel,
        grid_spec=pltpu.PrefetchScalarGridSpec(
            num_scalar_prefetch=1,
            grid=(len(blocks),),
            in_specs=[
                pl.BlockSpec((rows, width), lambda i, _: (0, 0), pipeline_mode=pl.Buffered(1))
            ]
            * len(blocks),
            out_specs=pl.BlockSpec((1, 1, rows, width), lambda i, at: (at[i, 0], at[i, 1], 0, 0)),
        ),
        out_shape=jax.ShapeDtypeStruct((n, 4, rows, width), blocks[0].dtype),
        compiler_params=pltpu.CompilerParams(vmem_limit_bytes=24 << 20),
        cost_estimate=pl.CostEstimate(
            flops=0, bytes_accessed=4 * len(blocks) * rows * width, transcendentals=0
        ),
        name="place_rows",
    )(jnp.stack([jnp.stack(at) for at in index]).astype(jnp.int32), *blocks)


def all_sum(v):
    v = v + core_swap(v)
    v = v + chip_swap(v)
    v = v + dp_swap(v)
    n = lax.axis_size("ctx")
    step = 1
    while step < n:
        v = v + lax.ppermute(v, "ctx", [(i, i ^ step) for i in range(n)])
        step *= 2
    return v


def norm_scale(v):
    return lax.rsqrt(jnp.mean(v * v, axis=-1, keepdims=True) + EPS)


def norm_back(v, r, gain, grad):
    z = v * r
    e = grad * gain
    return r * (e - z * jnp.mean(e * z, axis=-1, keepdims=True)), jnp.sum(grad * z, axis=(0, 1))


def slot_device(
    hidden_in,
    teacher,
    lengths,
    query_weight,
    key_weight,
    value_weight,
    out_weight,
    gate_weight,
    up_weight,
    down_weight,
    attention_gain,
    feed_gain,
):
    n_micro, n_slot, group, width = hidden_in.shape
    n_chunk = n_micro * n_slot
    quarter = group // 4
    cols = query_weight.shape[1]
    heads = cols // HEAD_DIM
    back = WINDOW // group
    ctx_index = lax.axis_index("ctx")
    dp_index = lax.axis_index("dp")
    mp_index = lax.axis_index("mp")
    core_index, x_index = mp_index % 2, mp_index // 2
    place = core_index * 2 + x_index
    share = attention_gain.shape[0]
    count = jnp.sum(lengths).astype(F32)
    factor = lengths.shape[0] * lengths.shape[1] * SEQ / count
    length = lax.dynamic_slice(
        lengths, (ctx_index // n_slot, dp_index * n_slot + ctx_index % n_slot), (1, 1)
    ).reshape(1)
    row = jnp.arange(group, dtype=jnp.int32)
    inside = ((row // quarter) ^ place) * quarter + row % quarter
    kcol, qrow = inside[:, None], inside[None, :]
    own_inside = place * quarter + jnp.arange(quarter, dtype=jnp.int32)
    chunks = range(n_chunk)

    def own_part(v):
        v = lax.dynamic_slice_in_dim(v.reshape(n_chunk, group, width), place * quarter, quarter, 1)
        return to_slots(own_first(v, dp_index), ctx_index)

    def by_chunk(parts):
        parts = jnp.stack(parts)
        return [pick(parts, (ctx_index - c) % n_chunk) for c in chunks]

    x_parts = own_part(hidden_in)
    x_peers = [chip_swap(part) for part in x_parts]
    x_pairs = [jnp.concatenate(pair, axis=0) for pair in zip(x_parts, x_peers)]
    x_cores = [core_swap(pair) for pair in x_pairs]
    x_own = by_chunk(x_parts)
    x_all = by_chunk([jnp.concatenate(pair, axis=0) for pair in zip(x_pairs, x_cores)])
    gain_rows = jnp.pad(jnp.stack([attention_gain, feed_gain]), ((0, 14), (0, cols - share)))
    shards = [
        jnp.concatenate([query_weight, gain_rows], axis=0),
        key_weight,
        value_weight,
        out_weight.T,
        gate_weight,
        up_weight,
    ]
    parts = []
    for i, shard in enumerate(shards):
        if i > 0:
            shard = after(shard, *x_parts, *parts[-2:-1])
        parts.append(lax.all_gather(shard, "ctx", axis=0, tiled=True))
    shard = after(down_weight.T, *x_parts, *parts[-2:-1])
    part_down = [
        lax.all_gather(v, "ctx", axis=0, tiled=True) for v in (shard, dp_swap(down_weight.T))
    ]
    gates = [x_parts, x_peers, x_cores] + [()] * 3
    fetched = [(part, dp_swap(after(part, *gate))) for part, gate in zip(parts, gates)]
    query_parts = [part.reshape(n_chunk, share + 16, cols) for part in fetched[0]]
    fetched[0] = [part[:, :share].reshape(n_chunk * share, cols) for part in query_parts]
    gain_a, gain_f = [
        jnp.concatenate([part[:, share + i, :share].reshape(-1) for part in query_parts]).astype(F32)
        for i in range(2)
    ]
    part_gate, part_up = parts[4:]
    w_query, w_key, w_value, w_out, w_gate, w_up = [
        jnp.concatenate(pair, axis=0) for pair in fetched
    ]
    teacher_parts = own_part(after(teacher, part_down[0]))
    target = by_chunk(teacher_parts)
    per = 2
    pairs = range(n_chunk // per)
    x_own = [jnp.stack(x_own[p * per : (p + 1) * per]) for p in pairs]
    target = [jnp.stack(target[p * per : (p + 1) * per]) for p in pairs]
    order = Order()
    reach = -(-back // per)
    mid, r_f, sent, kept = [], [], {}, {}

    def gather_half(own):
        return order(join, chip_swap(own), own)

    def gather_rest(pair):
        return order(join_flat, core_swap(pair), pair)

    def pass_core(p):
        sent[p], kept[p] = order(add_core, core_swap(sent[p]), kept[p])

    h1, queries, keys, values, attended, lse, h2 = [], [], [], [], [], [], []

    def project(h):
        return [plain_dot(h, w).astype(BF) for w in (w_query, w_key, w_value)]

    def normed(*xs):
        x = jnp.concatenate(xs, axis=0).astype(F32)
        return (x * norm_scale(x) * gain_a).astype(BF)

    def attention(p):
        first = max(0, p - reach)

        def step(q):
            ins = [q, *keys[first : p + 1], *values[first : p + 1]]
            shapes = [
                jax.ShapeDtypeStruct(q.shape, BF),
                jax.ShapeDtypeStruct((heads, per, group), F32),
            ]
            return attend_call(
                attend_kernel, "attend", p, per, back, kcol, qrow, length, ins, [], shapes, 24
            )

        a, l = order(step, queries[p])
        attended.append(a)
        lse.append(l)

    def enter_feed(p):
        def step(got, keep, x):
            v = x.astype(F32) + (keep + got.astype(F32))
            r = norm_scale(v)
            return (v * r * gain_f).astype(BF), v, r

        low, v, r = order(step, chip_swap(sent[p]), kept[p], x_own[p])
        mid.append(v)
        r_f.append(r)
        return low

    for p in pairs:
        h1.append(order(normed, *x_all[p * per : (p + 1) * per]))
    for p in pairs:
        q, k, v = order(project, h1[p])
        queries.append(q)
        keys.append(k)
        values.append(v)
        order.wait((parts[3], part_gate)[p])
        attention(p)
        sent[p], kept[p] = order(lambda a: split_part(right_dot(a, w_out), per), attended[p])
    pass_core(0)
    order.wait(fetched[4][1])
    pass_core(1)
    low = [enter_feed(0)]
    order.wait(part_up)
    low.append(enter_feed(1))
    low = [gather_half(v) for v in low]
    order.wait(fetched[5][1])
    h2.append(gather_rest(low[0]))

    gate, up, hidden, results, g_result, g_branch, loss_parts = [], [], [], [], [], [], []

    def unit(h):
        g, u = plain_dot(h, w_gate), plain_dot(h, w_up)
        return (g * jax.nn.sigmoid(g) * u).astype(BF), g, u

    def finish(p):
        def step(got, keep, v, t):
            at = (p * per + jnp.arange(per, dtype=jnp.int32))[:, None] * group + own_inside
            valid = (at < length)[:, :, None].astype(F32)
            result = (v + (keep + got.astype(F32))) * valid
            error = (result - t.astype(F32)) * valid
            grad = error * factor
            return grad.astype(BF), grad, result.astype(BF), jnp.sum(error * error)

        low, grad, result, loss = order(step, chip_swap(sent[p]), kept[p], mid[p], target[p])
        results.append(result)
        g_result.append(grad)
        loss_parts.append(loss)
        return low

    def feed(p):
        h, g, u = order(unit, h2[p])
        hidden.append(h)
        gate.append(g)
        up.append(u)

    def project_down(p):
        sent[p], kept[p] = order(lambda h: split_part(right_dot(h, w_down), per), hidden[p])

    g_gate, g_up, g_mid, g_att, gain_f_parts = [], [], [], [], []

    def leave_unit(p):
        def step(g_out, g, u):
            g_hidden = plain_dot(g_out, w_down)
            sig = jax.nn.sigmoid(g)
            return (
                (g_hidden * g * sig).astype(BF),
                (g_hidden * u * sig * (1.0 + g * (1.0 - sig))).astype(BF),
            )

        gu, gg = order(step, g_branch[p], gate[p], up[p])
        g_up.append(gu)
        g_gate.append(gg)

    def project_unit(p):
        def step(gg, gu):
            return split_part(right_dot(gg, w_gate) + right_dot(gu, w_up), per)

        sent[p], kept[p] = order(step, g_gate[p], g_up[p])

    def enter_attention(p):
        def step(got, keep, v, r, grad):
            g_norm, g_gain = norm_back(v, r, gain_f, keep + got.astype(F32))
            total = grad + g_norm
            return total.astype(BF), total, g_gain

        low, total, g_gain = order(step, chip_swap(sent[p]), kept[p], mid[p], r_f[p], g_result[p])
        g_mid.append(total)
        gain_f_parts.append(g_gain)
        return low

    scattered = []

    def scatter(rights, lefts, got):
        part = order(own_part_grad, rights[0], lefts[0])
        own = order(own_rest, rights[1], lefts[1], part, got)
        scattered.append(lax.psum_scatter(own, "ctx", scatter_dimension=0, tiled=True))

    def send(rights, lefts):
        part = order(their_part, rights[0], lefts[0])
        return dp_swap(order(their_rest, rights[1], lefts[1], part))

    g_q, g_k, g_v = [None] * len(pairs), [None] * len(pairs), [None] * len(pairs)
    g_in, gain_a_parts = [], []

    def attention_back(p):
        first = max(0, p - reach)
        last = p == len(pairs) - 1

        def step(g):
            ins = [queries[p], plain_dot(g, w_out).astype(BF), *keys[first : p + 1], *values[first : p + 1]]
            kinds = [BF if last or p - j == reach else F32 for j in range(first, p + 1)]
            shape = ins[0].shape
            shapes = [jax.ShapeDtypeStruct(shape, kind) for kind in [BF] + kinds * 2]
            return attend_call(
                attend_back_kernel, "attend_back", p, per, back, kcol, qrow, length,
                [*ins, *g_k[first:p], *g_v[first:p]], [lse[p]], shapes, 0,
            )

        out = order(step, g_att[p])
        n = p - first + 1
        g_q[p] = out[0]
        g_k[first : p + 1] = out[1 : 1 + n]
        g_v[first : p + 1] = out[1 + n :]

    def project_back(p):
        def step(q, k, v):
            whole = right_dot(q, w_query) + right_dot(k, w_key) + right_dot(v, w_value)
            return split_part(whole, per)

        sent[p], kept[p] = order(step, g_q[p], g_k[p], g_v[p])

    def leave(p):
        def step(got, keep, x, grad):
            x = x.astype(F32)
            g_norm, g_gain = norm_back(x, norm_scale(x), gain_a, keep + got.astype(F32))
            return (grad + g_norm).astype(BF), g_gain

        low, g_gain = order(step, chip_swap(sent[p]), kept[p], x_own[p], g_mid[p])
        g_in.append(low)
        gain_a_parts.append(g_gain)

    feed(0)
    w_down = jnp.concatenate([part_down[0], after(part_down[1], hidden[0])], axis=0)
    order.wait(*teacher_parts)
    project_down(0)
    h2.append(gather_rest(low[1]))
    pass_core(0)
    feed(1)
    first = finish(0)
    project_down(1)
    pass_core(1)
    g_branch.append(gather_rest(gather_half(first)))
    leave_unit(0)
    part = order(whole_part, hidden[0], g_branch[0])
    second = finish(1)
    out_parts = to_slots(own_first(jnp.concatenate(results, axis=0), dp_index), ctx_index)
    project_unit(0)
    pass_core(0)
    order.wait(*out_parts)
    g_branch.append(gather_rest(gather_half(second)))
    leave_unit(1)
    s_down = both_scatter(order(whole_rest, hidden[1], g_branch[1], part))
    first = enter_attention(0)
    project_unit(1)
    pass_core(1)
    part = order(whole_part, g_gate[0], h2[0])
    s_gate = both_scatter(order(whole_rest, g_gate[1], h2[1], part))
    g_att.append(gather_rest(gather_half(first)))
    attention_back(0)
    order.wait(s_down)
    second = enter_attention(1)
    g_att.append(gather_rest(gather_half(second)))
    part = order(whole_part, g_up[0], h2[0])
    s_up = both_scatter(order(whole_rest, g_up[1], h2[1], part))
    out_got = send(attended, g_att)
    out_own = order(lambda first, *rest: jnp.stack([first, *rest]), *out_parts)
    out_peer, out_core = chip_swap(out_own), core_swap(out_own)
    attention_back(1)
    order.wait(out_peer, out_got)
    project_back(0)
    pass_core(0)
    rights = [
        order(lambda q, k, v: jnp.concatenate([q, k, v], axis=1), g_q[p], g_k[p], g_v[p]) for p in pairs
    ]
    qkv_got = send(rights, h1)
    order.wait(s_gate)
    project_back(1)
    leave(0)
    pass_core(1)
    leave(1)
    back_parts = to_slots(own_first(jnp.concatenate(g_in, axis=0), dp_index), ctx_index)
    scatter(attended, g_att, out_got)
    part = order(own_part_grad, rights[0], h1[0])
    slots = [(ctx_index - k) % n_chunk for k in chunks]
    index = [(slot, place ^ i) for slot in slots for i in range(4)]

    def place_out(own, *others):
        blocks = [v[k] for k in chunks for v in (own, *others)]
        return whole_rows(blocks, index, n_chunk)

    order.wait(*back_parts, qkv_got)
    out_hidden = order(place_out, out_own, out_peer, out_core, core_swap(out_peer))
    back_peers = [chip_swap(own) for own in back_parts]
    order.wait(s_up, *back_peers)
    own = order(own_rest, rights[1], h1[1], part, qkv_got)
    s_qkv = lax.psum_scatter(own, "ctx", scatter_dimension=0, tiled=True).astype(F32)
    back_blocks = []
    for own, peer in zip(back_parts, back_peers):
        back_blocks += [own, peer, core_swap(own), core_swap(peer)]
    grad_hidden = order(lambda first, *rest: whole_rows([first, *rest], index, n_chunk), *back_blocks)
    grad_down, grad_gate, grad_up = [v.astype(F32) for v in (s_down, s_gate, s_up)]
    gain_a_part, gain_f_part, loss_part = sum(gain_a_parts), sum(gain_f_parts), sum(loss_parts)
    small = jnp.concatenate(
        [own_first(gain_a_part, dp_index), own_first(gain_f_part, dp_index), jnp.full((128,), loss_part)]
    )
    small = all_sum(after(small, *back_peers).reshape(-1, 128)).reshape(-1)
    at = (dp_index * n_chunk + ctx_index) * share
    shape = hidden_in.shape
    return (
        out_hidden.reshape(shape),
        small[2 * width] / (count * width),
        grad_hidden.reshape(shape),
        s_qkv[:, :cols],
        s_qkv[:, cols : 2 * cols],
        s_qkv[:, 2 * cols :],
        scattered[0].astype(F32).T,
        grad_gate,
        grad_up,
        grad_down.T,
        lax.dynamic_slice_in_dim(small, at, share),
        lax.dynamic_slice_in_dim(small, width + at, share),
    )


def shifted(value, axis, steps):
    count = lax.axis_size(axis)
    leading, last = (max(0, -steps), min(count, count - steps))
    return lax.ppermute(value, axis, [(source, source + steps) for source in range(leading, last)])


def norm_rows(v):
    return v * lax.rsqrt(jnp.mean(v * v, axis=-1, keepdims=True) + EPS)


def silu(v):
    return v * jax.nn.sigmoid(v)


def gain_norm(values, gain):
    return norm_rows(values) * gain


def gated_unit(gate, upper):
    return silu(gate) * upper


def on_device(
    hidden_in,
    teacher,
    lengths,
    query_weight,
    key_weight,
    value_weight,
    out_weight,
    gate_weight,
    up_weight,
    down_weight,
    attention_gain,
    feed_gain,
):
    n_micro, n_slot, group, width = hidden_in.shape
    local_heads = query_weight.shape[1] // HEAD_DIM
    head_cols = query_weight.shape[1]
    reach = WINDOW // group
    extent = (reach + 1) * group
    rows = n_slot * group
    scale = HEAD_DIM ** (-0.5)
    ctx_index = lax.axis_index("ctx")
    dp_index = lax.axis_index("dp")
    count = jnp.sum(lengths).astype(jnp.float32)
    factor = lengths.shape[0] * lengths.shape[1] * SEQ / count
    own_lengths = lax.dynamic_slice_in_dim(lengths, dp_index * n_slot, n_slot, 1)
    positions = ctx_index * group + jnp.arange(group, dtype=jnp.int32)
    key_positions = ctx_index * group - reach * group + jnp.arange(extent, dtype=jnp.int32)
    distance = positions[:, None] - key_positions[None, :]
    in_window = (distance >= 0) & (distance < WINDOW) & (key_positions[None, :] >= 0)

    def fetch_attention():
        return (
            lax.all_gather(query_weight, ("dp", "ctx"), axis=0, tiled=True),
            lax.all_gather(key_weight, ("dp", "ctx"), axis=0, tiled=True),
            lax.all_gather(value_weight, ("dp", "ctx"), axis=0, tiled=True),
            lax.all_gather(out_weight, ("dp", "ctx"), axis=1, tiled=True),
            lax.all_gather(attention_gain, ("dp", "ctx"), axis=0, tiled=True),
        )

    def fetch_feed():
        return (
            lax.all_gather(gate_weight, ("dp", "ctx"), axis=0, tiled=True),
            lax.all_gather(up_weight, ("dp", "ctx"), axis=0, tiled=True),
            lax.all_gather(down_weight, ("dp", "ctx"), axis=1, tiled=True),
            lax.all_gather(feed_gain, ("dp", "ctx"), axis=0, tiled=True),
        )

    acc_query = jnp.zeros((width, head_cols), jnp.float32)
    acc_key = jnp.zeros((width, head_cols), jnp.float32)
    acc_value = jnp.zeros((width, head_cols), jnp.float32)
    acc_out = jnp.zeros((head_cols, width), jnp.float32)
    acc_gate = jnp.zeros((width, gate_weight.shape[1]), jnp.float32)
    acc_up = jnp.zeros((width, gate_weight.shape[1]), jnp.float32)
    acc_down = jnp.zeros((gate_weight.shape[1], width), jnp.float32)
    acc_gain_a = jnp.zeros((width,), jnp.float32)
    acc_gain_f = jnp.zeros((width,), jnp.float32)
    loss_part = jnp.zeros((), jnp.float32)
    results = []
    input_grads = []

    def scores_of(queries_four, keys_ext, allowed):
        raw = (
            jnp.einsum(
                "sqhd,skhd->shqk", queries_four, keys_ext, preferred_element_type=jnp.float32
            )
            * scale
        )
        return jnp.where(allowed[:, None], raw, NEGATIVE)

    for micro in range(n_micro):
        slot_len = own_lengths[micro]
        valid = positions[None, :] < slot_len[:, None]
        key_ok = (key_positions[None, None, :] < slot_len[:, None, None]) | (distance == 0)[None]
        allowed = in_window[None] & key_ok
        valid_rows = valid.reshape(rows, 1).astype(jnp.float32)
        attention_set = fetch_attention()
        full_query, full_key, full_value, full_out, full_gain_a = attention_set
        gain_a = full_gain_a.astype(jnp.float32)
        x_in = hidden_in[micro].reshape(rows, width).astype(jnp.float32)
        normed_a = gain_norm(x_in, gain_a).astype(jnp.bfloat16)
        queries = plain_dot(normed_a, full_query).astype(jnp.bfloat16)
        keys = plain_dot(normed_a, full_key).astype(jnp.bfloat16)
        values = plain_dot(normed_a, full_value).astype(jnp.bfloat16)
        keys_slot = keys.reshape(n_slot, group, head_cols)
        values_slot = values.reshape(n_slot, group, head_cols)
        key_parts = []
        value_parts = []
        for back in range(reach, 0, -1):
            got_keys, got_values = shifted((keys_slot, values_slot), "ctx", back)
            key_parts.append(got_keys)
            value_parts.append(got_values)
        keys_ext = jnp.concatenate(key_parts + [keys_slot], axis=1).reshape(
            n_slot, extent, local_heads, HEAD_DIM
        )
        values_ext = jnp.concatenate(value_parts + [values_slot], axis=1).reshape(
            n_slot, extent, local_heads, HEAD_DIM
        )
        queries_four = queries.reshape(n_slot, group, local_heads, HEAD_DIM)
        scores = scores_of(queries_four, keys_ext, allowed)
        top = jnp.max(scores, axis=-1, keepdims=True)
        expo = jnp.exp(scores - top)
        summed = jnp.sum(expo, axis=-1, keepdims=True)
        logsum = top + jnp.log(summed)
        probs = (expo / summed).astype(jnp.bfloat16)
        attended = jnp.einsum(
            "shqk,skhd->sqhd", probs, values_ext, preferred_element_type=jnp.float32
        )
        attended = attended.astype(jnp.bfloat16).reshape(rows, head_cols)
        branch_a = lax.psum(plain_dot(attended, full_out), "mp")
        mid = x_in + branch_a
        feed_set = fetch_feed()
        full_gate, full_up, full_down, full_gain_f = feed_set
        gain_f = full_gain_f.astype(jnp.float32)
        normed_f = gain_norm(mid, gain_f).astype(jnp.bfloat16)
        gate_val = plain_dot(normed_f, full_gate)
        up_val = plain_dot(normed_f, full_up)
        hidden_units = gated_unit(gate_val, up_val).astype(jnp.bfloat16)
        branch_f = lax.psum(plain_dot(hidden_units, full_down), "mp")
        result = (mid + branch_f) * valid_rows
        target = teacher[micro].reshape(rows, width).astype(jnp.float32)
        error = (result - target) * valid_rows
        loss_part = loss_part + jnp.sum(error * error)
        results.append(result.astype(jnp.bfloat16).reshape(n_slot, group, width))
        back_feed = fetch_feed()
        full_gate, full_up, full_down, full_gain_f = back_feed
        grad_result = error * factor
        grad_branch = grad_result.astype(jnp.bfloat16)
        acc_down = acc_down + left_dot(hidden_units, grad_branch)
        grad_units = right_dot(grad_branch, full_down)
        unused, pull_unit = jax.vjp(gated_unit, gate_val, up_val)
        grad_gate, grad_upper = pull_unit(grad_units)
        grad_gate = grad_gate.astype(jnp.bfloat16)
        grad_upper = grad_upper.astype(jnp.bfloat16)
        acc_gate = acc_gate + left_dot(normed_f, grad_gate)
        acc_up = acc_up + left_dot(normed_f, grad_upper)
        grad_normed_f = lax.psum(
            right_dot(grad_gate, full_gate) + right_dot(grad_upper, full_up), "mp"
        )
        unused, pull_norm = jax.vjp(gain_norm, mid, gain_f)
        grad_mid_norm, grad_gain_f = pull_norm(grad_normed_f)
        acc_gain_f = acc_gain_f + grad_gain_f
        grad_mid = grad_result + grad_mid_norm
        back_attention = fetch_attention()
        full_query, full_key, full_value, full_out, full_gain_a = back_attention
        grad_att = grad_mid.astype(jnp.bfloat16)
        acc_out = acc_out + left_dot(attended, grad_att)
        grad_attended = (
            right_dot(grad_att, full_out)
            .astype(jnp.bfloat16)
            .reshape(n_slot, group, local_heads, HEAD_DIM)
        )
        scores_again = scores_of(queries_four, keys_ext, allowed)
        probs_back = jnp.exp(scores_again - logsum)
        grad_values_ext = jnp.einsum(
            "shqk,sqhd->skhd",
            probs_back.astype(jnp.bfloat16),
            grad_attended,
            preferred_element_type=jnp.float32,
        )
        grad_probs = jnp.einsum(
            "sqhd,skhd->shqk", grad_attended, values_ext, preferred_element_type=jnp.float32
        )
        inner = jnp.sum(probs_back * grad_probs, axis=-1, keepdims=True)
        grad_scores = (probs_back * (grad_probs - inner)).astype(jnp.bfloat16)
        grad_queries = (
            jnp.einsum("shqk,skhd->sqhd", grad_scores, keys_ext, preferred_element_type=jnp.float32)
            * scale
        )
        grad_keys_ext = (
            jnp.einsum(
                "shqk,sqhd->skhd", grad_scores, queries_four, preferred_element_type=jnp.float32
            )
            * scale
        )
        grad_keys_ext = grad_keys_ext.reshape(n_slot, extent, head_cols)
        grad_values_ext = grad_values_ext.reshape(n_slot, extent, head_cols)
        grad_keys_total = grad_keys_ext[:, reach * group :]
        grad_values_total = grad_values_ext[:, reach * group :]
        for back in range(1, reach + 1):
            offset = (reach - back) * group
            piece_keys = grad_keys_ext[:, offset : offset + group]
            piece_values = grad_values_ext[:, offset : offset + group]
            got_keys, got_values = shifted((piece_keys, piece_values), "ctx", -back)
            grad_keys_total = grad_keys_total + got_keys
            grad_values_total = grad_values_total + got_values
        grad_queries = grad_queries.reshape(rows, head_cols).astype(jnp.bfloat16)
        grad_keys_low = grad_keys_total.reshape(rows, head_cols).astype(jnp.bfloat16)
        grad_values_low = grad_values_total.reshape(rows, head_cols).astype(jnp.bfloat16)
        acc_query = acc_query + left_dot(normed_a, grad_queries)
        acc_key = acc_key + left_dot(normed_a, grad_keys_low)
        acc_value = acc_value + left_dot(normed_a, grad_values_low)
        grad_normed_a = (
            right_dot(grad_queries, full_query)
            + right_dot(grad_keys_low, full_key)
            + right_dot(grad_values_low, full_value)
        )
        grad_normed_a = lax.psum(grad_normed_a, "mp")
        unused, pull_first = jax.vjp(gain_norm, x_in, gain_a)
        grad_x_norm, grad_gain_a = pull_first(grad_normed_a)
        acc_gain_a = acc_gain_a + grad_gain_a
        grad_in = grad_mid + grad_x_norm
        input_grads.append(grad_in.astype(jnp.bfloat16).reshape(n_slot, group, width))
    loss = lax.psum(loss_part, ("dp", "ctx")) / (count * width)
    grads = (
        lax.psum_scatter(acc_query, ("dp", "ctx"), scatter_dimension=0, tiled=True),
        lax.psum_scatter(acc_key, ("dp", "ctx"), scatter_dimension=0, tiled=True),
        lax.psum_scatter(acc_value, ("dp", "ctx"), scatter_dimension=0, tiled=True),
        lax.psum_scatter(acc_out, ("dp", "ctx"), scatter_dimension=1, tiled=True),
        lax.psum_scatter(acc_gate, ("dp", "ctx"), scatter_dimension=0, tiled=True),
        lax.psum_scatter(acc_up, ("dp", "ctx"), scatter_dimension=0, tiled=True),
        lax.psum_scatter(acc_down, ("dp", "ctx"), scatter_dimension=1, tiled=True),
        lax.psum_scatter(acc_gain_a, ("dp", "ctx"), scatter_dimension=0, tiled=True),
        lax.psum_scatter(acc_gain_f, ("dp", "ctx"), scatter_dimension=0, tiled=True),
    )
    return (
        jnp.stack(results),
        loss,
        jnp.stack(input_grads),
        grads[0],
        grads[1],
        grads[2],
        grads[3],
        grads[4],
        grads[5],
        grads[6],
        grads[7],
        grads[8],
    )


def solution(mesh):
    in_specs = (
        P(None, "dp", "ctx", None),
        P(None, "dp", "ctx", None),
        P(),
        P(("dp", "ctx"), "mp"),
        P(("dp", "ctx"), "mp"),
        P(("dp", "ctx"), "mp"),
        P("mp", ("dp", "ctx")),
        P(("dp", "ctx"), "mp"),
        P(("dp", "ctx"), "mp"),
        P("mp", ("dp", "ctx")),
        P(("dp", "ctx")),
        P(("dp", "ctx")),
    )
    out_specs = (
        P(None, "dp", "ctx", None),
        P(),
        P(None, "dp", "ctx", None),
        P(("dp", "ctx"), "mp"),
        P(("dp", "ctx"), "mp"),
        P(("dp", "ctx"), "mp"),
        P("mp", ("dp", "ctx")),
        P(("dp", "ctx"), "mp"),
        P(("dp", "ctx"), "mp"),
        P("mp", ("dp", "ctx")),
        P(("dp", "ctx")),
        P(("dp", "ctx")),
    )
    slots = 8 // mesh.shape["dp"]
    whole_slots = mesh.shape["ctx"] == slots and mesh.shape["mp"] == 4
    return jax.shard_map(
        slot_device if whole_slots else on_device, mesh=mesh, in_specs=in_specs, out_specs=out_specs, check_vma=False
    )
```
